256 devices in a mesh: slab: 64 (over x, y, z_hi), col: 4 (over z_lo, core).
Axes of the slice: x: 4, y: 4, z: 8 (z_hi: 4, z_lo: 2; z = z_hi * 2 + z_lo), core: 2. Of those that a mesh axis runs over, the one named last changes fastest.
Arguments:
- psi0: bfloat16 [256, 256, 1024], P('col', 'slab'), may hold values from -4 to 4
- onsite: float32 [256, 1024], P('slab'), may hold values from -0.4 to 0.4
- hop_x: float32 [256, 1024], P('slab'), may hold values from 0.12 to 0.36
- hop_y: float32 [256, 1024], P('slab'), may hold values from 0.12 to 0.36
- cos_coef: float32 [8, 3], replicated, may hold values from -1 to 1
- sin_coef: float32 [8, 3], replicated, may hold values from -1 to 1
Outputs:
- currents: float32 [8, 2, 256, 1024], P(None, None, 'slab', 'col')
The draws below stay inside these ranges and needn't reach their ends.
All inputs are finite; a program needn't handle non-finite values.
Results may differ from the reference program's by a relative error of at most 0.0051.
Values may be sent and summed in bfloat16 or wider, within the bound.
A program may use at most 128 MiB of HBM per device.

```python
import math
import jax
import jax.numpy as jnp
from jax import lax

W = 1024
C_DEV = 64
NE = 8
NX = 256
COLS = 256


def draw_psi0(key, part):
    key_scale, key_base = jax.random.split(key, 2)
    col_scale = jnp.exp(jax.random.uniform(key_scale, (COLS, 1, 1), jnp.float32, math.log(0.2), math.log(2.0)))
    values = col_scale * 0.5 * jax.random.normal(key_base, (COLS, NX, W), jnp.float32)
    return jnp.clip(values, -4.0, 4.0).astype(jnp.bfloat16)


def level_of(own_key, dims, shards, smallest, high):
    gain, own = 1.0, jax.random.fold_in(own_key, 6)
    for position, shards_of in shards:
        draws = jnp.exp(jax.random.uniform(jax.random.fold_in(own, position), (shards_of,), jnp.float32, smallest / len(shards), high / len(shards)))
        gain = gain * jnp.repeat(draws, dims[position] // shards_of).reshape([-1 if axis == position else 1 for axis in range(len(dims))])
    return gain


def setup_inputs(seed: int = 0) -> dict:
    key_list = jax.random.split(jax.random.key(seed), 7)
    return {
        "psi0": draw_psi0(jax.random.fold_in(key_list[6], 71), 0),
        "onsite": jnp.clip(jax.random.uniform(key_list[1], (NX, W), jnp.float32, -0.4, 0.4) * level_of(key_list[1], (NX, W), ((0, 64),), -0.4, 0.0), -0.4, 0.4),
        "hop_x": jnp.clip(jnp.exp(math.log(0.36) - 1.09861235 * jax.random.uniform(key_list[2], (NX, W), jnp.float32) ** level_of(key_list[2], (NX, W), ((0, 64),), -0.2, 0.2)), 0.12, 0.36),
        "hop_y": jnp.clip(jnp.exp(math.log(0.36) - 1.09861235 * jax.random.uniform(key_list[3], (NX, W), jnp.float32) ** level_of(key_list[3], (NX, W), ((0, 64),), -0.2, 0.2)), 0.12, 0.36),
        "cos_coef": jnp.clip(jax.random.uniform(key_list[4], (NE, 3), jnp.float32, -1.0, 1.0), -1.0, 1.0),
        "sin_coef": jnp.clip(jax.random.uniform(key_list[5], (NE, 3), jnp.float32, -1.0, 1.0), -1.0, 1.0),
    }


def masked_bonds(hop_y):
    rows_index = jnp.arange(NX, dtype=jnp.int32)[:, None]
    site_index = jnp.arange(W, dtype=jnp.int32)[None, :]
    keep = ((rows_index + site_index) % 2 == 0) & (site_index < W - 1)
    return jnp.where(keep, hop_y, jnp.float32(0.0))


def apply_ham(field, onsite, hop_x, hop_ym):
    values = field.astype(jnp.float32)
    batch = values.shape[0]
    zero_row = jnp.zeros((batch, 1, W), jnp.float32)
    below = jnp.concatenate([zero_row, values[:, :-1]], axis=1)
    above = jnp.concatenate([values[:, 1:], zero_row], axis=1)
    hop_below = jnp.concatenate([jnp.zeros((1, W), jnp.float32), hop_x[:-1]], axis=0)
    zero_col = jnp.zeros((batch, NX, 1), jnp.float32)
    right = jnp.concatenate([values[:, :, 1:], zero_col], axis=2)
    left = jnp.concatenate([zero_col, values[:, :, :-1]], axis=2)
    hop_left = jnp.concatenate([jnp.zeros((NX, 1), jnp.float32), hop_ym[:, :-1]], axis=1)
    return onsite * values - hop_below * below - hop_x * above - hop_ym * right - hop_left * left


def reference(psi0, onsite, hop_x, hop_y, cos_coef, sin_coef):
    hop_ym = masked_bonds(hop_y)
    block_cols = C_DEV // 4
    blocks = psi0.reshape(COLS // block_cols, block_cols, NX, W)

    def one_block(total, block):
        first = apply_ham(block, onsite, hop_x, hop_ym).astype(jnp.bfloat16)
        second = (2.0 * apply_ham(first, onsite, hop_x, hop_ym) - block.astype(jnp.float32)).astype(jnp.bfloat16)
        vectors = (block.astype(jnp.float32), first.astype(jnp.float32), second.astype(jnp.float32))
        zero_row = jnp.zeros((block.shape[0], 1, W), jnp.float32)
        zero_col = jnp.zeros((block.shape[0], NX, 1), jnp.float32)
        maps = []
        for energy in range(NE):
            u_state = cos_coef[energy, 0] * vectors[0] + cos_coef[energy, 1] * vectors[1] + cos_coef[energy, 2] * vectors[2]
            v_state = sin_coef[energy, 0] * vectors[0] + sin_coef[energy, 1] * vectors[1] + sin_coef[energy, 2] * vectors[2]
            u_up = jnp.concatenate([u_state[:, 1:], zero_row], axis=1)
            v_up = jnp.concatenate([v_state[:, 1:], zero_row], axis=1)
            u_right = jnp.concatenate([u_state[:, :, 1:], zero_col], axis=2)
            v_right = jnp.concatenate([v_state[:, :, 1:], zero_col], axis=2)
            along = hop_x * jnp.sum(u_state * v_up - v_state * u_up, axis=0)
            across = hop_ym * jnp.sum(u_state * v_right - v_state * u_right, axis=0)
            maps.append(jnp.stack([along, across]))
        return total + jnp.stack(maps), None

    start = jnp.zeros((NE, 2, NX, W), jnp.float32)
    total, unused = lax.scan(one_block, start, blocks)
    return total
```

```python
import functools

import jax
import jax.numpy as jnp
from jax import lax
from jax.experimental import pallas as pl
from jax.experimental.pallas import tpu as pltpu
from jax.sharding import PartitionSpec as P

MESH = pl.DeviceIdType.MESH
CHUNKS = 8
STEP = 2


def kernel(slabs, cols, psi, onsite, hop_x, hop_y, cos_ref, sin_ref, out,
           field, to_up, to_down, from_down, from_up, coef, acc, part, extra,
           got, got_extra, local_sem, send_sem, recv_sem, coef_send, coef_recv,
           part_send, part_recv, extra_send, extra_recv):
    slab = lax.axis_index("slab")
    col = lax.axis_index("col")
    batch, rows, width = psi.shape
    per = batch // CHUNKS
    quarter = width // cols
    has_down = slab > 0
    has_up = slab < slabs - 1

    def span(i):
        return pl.ds(i * per, per)

    def local(i):
        return pltpu.make_async_copy(
            psi.at[span(i)], field.at[span(i), 2:6, :], local_sem.at[i])

    def upward(i):
        return pltpu.make_async_remote_copy(
            src_ref=psi.at[span(i), 2:4, :], dst_ref=field.at[span(i), 0:2, :],
            send_sem=send_sem.at[0, i], recv_sem=recv_sem.at[0, i],
            device_id=(slab + 1, col), device_id_type=MESH)

    def downward(i):
        return pltpu.make_async_remote_copy(
            src_ref=psi.at[span(i), 0:2, :], dst_ref=field.at[span(i), 6:8, :],
            send_sem=send_sem.at[1, i], recv_sem=recv_sem.at[1, i],
            device_id=(slab - 1, col), device_id_type=MESH)

    coef_up = pltpu.make_async_remote_copy(
        src_ref=to_up, dst_ref=from_down, send_sem=coef_send.at[0],
        recv_sem=coef_recv.at[0], device_id=(slab + 1, col), device_id_type=MESH)
    coef_down = pltpu.make_async_remote_copy(
        src_ref=to_down, dst_ref=from_up, send_sem=coef_send.at[1],
        recv_sem=coef_recv.at[1], device_id=(slab - 1, col), device_id_type=MESH)

    for i in range(CHUNKS):
        local(i).start()

    barrier = pltpu.get_barrier_semaphore()
    for by in range(1, cols):
        pl.semaphore_signal(barrier, inc=1, device_id=(slab, lax.rem(col + by, cols)),
                            device_id_type=MESH)

    @pl.when(has_up)
    def _():
        for other in range(cols):
            pl.semaphore_signal(barrier, inc=1, device_id=(slab + 1, other), device_id_type=MESH)

    @pl.when(has_down)
    def _():
        for other in range(cols):
            pl.semaphore_signal(barrier, inc=1, device_id=(slab - 1, other), device_id_type=MESH)

    zero = jnp.zeros((1, width), jnp.float32)
    to_up[...] = jnp.concatenate(
        [hop_x[2:4, :], onsite[3:4, :], hop_y[3:4, :]], axis=0)
    to_down[...] = jnp.concatenate(
        [hop_x[0:1, :], onsite[0:1, :], hop_y[0:1, :], zero], axis=0)

    sides = jnp.where(has_up, 1, 0) + jnp.where(has_down, 1, 0)
    pl.semaphore_wait(barrier, cols - 1 + cols * sides)

    @pl.when(has_up)
    def _():
        coef_up.start()

    @pl.when(has_down)
    def _():
        coef_down.start()

    for i in range(CHUNKS):
        @pl.when(has_up)
        def _():
            upward(i).start()

        @pl.when(has_down)
        def _():
            downward(i).start()

    blank = jnp.zeros((batch, 2, width), jnp.bfloat16)

    @pl.when(jnp.logical_not(has_down))
    def _():
        field[:, 0:2, :] = blank
        from_down[...] = jnp.zeros_like(from_down)

    @pl.when(jnp.logical_not(has_up))
    def _():
        field[:, 6:8, :] = blank
        from_up[...] = jnp.zeros_like(from_up)

    acc[...] = jnp.zeros_like(acc)

    @pl.when(has_down)
    def _():
        coef_up.wait_recv()

    @pl.when(has_up)
    def _():
        coef_down.wait_recv()

    low = from_down[...]
    high = from_up[...]
    site_x = jnp.concatenate([low[0:2], hop_x[...], high[0:1], zero], axis=0)
    site_on = jnp.concatenate([zero, low[2:3], onsite[...], high[1:2], zero], axis=0)
    site_y = jnp.concatenate([zero, low[3:4], hop_y[...], high[2:3], zero], axis=0)
    row_id = lax.broadcasted_iota(jnp.int32, (8, width), 0)
    lane_id = lax.broadcasted_iota(jnp.int32, (8, width), 1)
    even = lax.rem(row_id + lane_id, 2) == 0
    site_x = jnp.where((row_id == 5) & jnp.logical_not(has_up), 0.0, site_x)
    bond_y = jnp.where(even & (lane_id < width - 1), site_y, 0.0)
    coef[0] = site_on
    coef[1] = pltpu.roll(site_x, 1, 0)
    coef[2] = site_x
    coef[3] = bond_y + pltpu.roll(bond_y, 1, 1)

    def partner(f):
        return jnp.where(even, pltpu.roll(f, width - 1, 1), pltpu.roll(f, 1, 1))

    def hamiltonian(f, above, beside):
        return coef[0] * f - coef[1] * pltpu.roll(f, 1, 0) - coef[2] * above - coef[3] * beside

    def one(c):
        p = field[c].astype(jnp.float32)
        p_up = pltpu.roll(p, 7, 0)
        p_side = partner(p)
        q = hamiltonian(p, p_up, p_side).astype(jnp.bfloat16).astype(jnp.float32)
        q_up = pltpu.roll(q, 7, 0)
        q_side = partner(q)
        t = (2.0 * hamiltonian(q, q_up, q_side) - p).astype(jnp.bfloat16).astype(jnp.float32)
        t_up = pltpu.roll(t, 7, 0)
        t_side = partner(t)
        return (
            p * q_up - q * p_up, p * t_up, t * p_up, q * t_up, t * q_up,
            p * q_side - q * p_side, p * t_side - t * p_side, q * t_side - t * q_side)

    def chunk(i, carry):
        local(i).wait()

        @pl.when(has_down)
        def _():
            upward(i).wait_recv()

        @pl.when(has_up)
        def _():
            downward(i).wait_recv()

        def columns(j, inner):
            first = i * per + j * STEP
            terms = one(first)
            for k in range(1, STEP):
                terms = [a + b for a, b in zip(terms, one(first + k))]
            for n, term in enumerate(terms):
                acc[n] += term
            return inner

        return lax.fori_loop(0, per // STEP, columns, carry)

    lax.fori_loop(0, CHUNKS, chunk, 0)

    first_half = row_id < 4

    def packed(along, across):
        return jnp.where(first_half, pltpu.roll(along, 6, 0), pltpu.roll(across, 2, 0))

    top = row_id == 5
    whole = (
        packed(acc[0], acc[5]),
        packed(jnp.where(top, 0.0, acc[1]) - acc[2], acc[6]),
        packed(jnp.where(top, 0.0, acc[3]) - acc[4], acc[7]))
    for k in range(3):
        for j in range(cols):
            part[j, k] = whole[k][:, j * quarter:(j + 1) * quarter]
    two = jnp.concatenate([acc[1, 1:2, :], acc[3, 1:2, :]], axis=0)
    for j in range(cols):
        extra[j] = two[:, j * quarter:(j + 1) * quarter]

    def to_peer(by):
        peer = lax.rem(col + by, cols)
        return pltpu.make_async_remote_copy(
            src_ref=part.at[peer], dst_ref=got.at[by - 1], send_sem=part_send.at[by - 1],
            recv_sem=part_recv.at[by - 1], device_id=(slab, peer), device_id_type=MESH)

    def to_below(by):
        peer = lax.rem(col + by, cols)
        return pltpu.make_async_remote_copy(
            src_ref=extra.at[peer], dst_ref=got_extra.at[by], send_sem=extra_send.at[by],
            recv_sem=extra_recv.at[by], device_id=(slab - 1, peer), device_id_type=MESH)

    for by in range(1, cols):
        to_peer(by).start()

    @pl.when(has_down)
    def _():
        for by in range(cols):
            to_below(by).start()

    @pl.when(jnp.logical_not(has_up))
    def _():
        got_extra[...] = jnp.zeros_like(got_extra)

    for by in range(1, cols):
        to_peer(by).wait_recv()

    @pl.when(has_up)
    def _():
        for by in range(cols):
            to_below(by).wait_recv()

    here = pl.ds(pl.multiple_of(col * quarter, quarter), quarter)
    extra_sum = got_extra[0] + got_extra[1] + got_extra[2] + got_extra[3]
    own_x = hop_x[:, here]
    own_y = hop_y[:, here]
    row4 = lax.broadcasted_iota(jnp.int32, (4, quarter), 0)
    lane4 = lax.broadcasted_iota(jnp.int32, (4, quarter), 1)
    keep = (lax.rem(row4 + lane4, 2) == 0) & (lane4 + col * quarter < width - 1)
    own_y = jnp.where(keep, own_y, 0.0)
    along = []
    across = []
    for k in range(3):
        total = part[col, k] + got[0, k] + got[1, k] + got[2, k]
        a = total[0:4]
        if k:
            a = a + jnp.where(row4 == 3, extra_sum[k - 1:k], 0.0)
        along.append(a * own_x)
        across.append(total[4:8] * own_y)
    for e in range(cos_ref.shape[1]):
        c0, c1, c2 = (cos_ref[n, e] for n in range(3))
        s0, s1, s2 = (sin_ref[n, e] for n in range(3))
        d = (c0 * s1 - c1 * s0, c0 * s2 - c2 * s0, c1 * s2 - c2 * s1)
        out[e, 0] = d[0] * along[0] + d[1] * along[1] + d[2] * along[2]
        out[e, 1] = d[0] * across[0] + d[1] * across[1] + d[2] * across[2]

    @pl.when(has_up)
    def _():
        coef_up.wait_send()
        for i in range(CHUNKS):
            upward(i).wait_send()

    @pl.when(has_down)
    def _():
        coef_down.wait_send()
        for i in range(CHUNKS):
            downward(i).wait_send()
        for by in range(cols):
            to_below(by).wait_send()

    for by in range(1, cols):
        to_peer(by).wait_send()


def solution(mesh):
    slabs, cols = mesh.shape["slab"], mesh.shape["col"]

    def on_device(psi0, onsite, hop_x, hop_y, cos_coef, sin_coef):
        batch, rows, width = psi0.shape
        quarter = width // cols
        vmem = pl.BlockSpec(memory_space=pltpu.VMEM)
        smem = pl.BlockSpec(memory_space=pltpu.SMEM)
        f32 = jnp.float32
        return pl.pallas_call(
            functools.partial(kernel, slabs, cols),
            out_shape=jax.ShapeDtypeStruct((cos_coef.shape[0], 2, rows, quarter), f32),
            in_specs=[pl.BlockSpec(memory_space=pl.ANY), vmem, vmem, vmem, smem, smem],
            out_specs=vmem,
            scratch_shapes=[
                pltpu.VMEM((batch, 8, width), jnp.bfloat16),
                pltpu.VMEM((4, width), f32),
                pltpu.VMEM((4, width), f32),
                pltpu.VMEM((4, width), f32),
                pltpu.VMEM((4, width), f32),
                pltpu.VMEM((4, 8, width), f32),
                pltpu.VMEM((8, 8, width), f32),
                pltpu.VMEM((cols, 3, 8, quarter), f32),
                pltpu.VMEM((cols, 2, quarter), f32),
                pltpu.VMEM((cols - 1, 3, 8, quarter), f32),
                pltpu.VMEM((cols, 2, quarter), f32),
                pltpu.SemaphoreType.DMA((CHUNKS,)),
                pltpu.SemaphoreType.DMA((2, CHUNKS)),
                pltpu.SemaphoreType.DMA((2, CHUNKS)),
                pltpu.SemaphoreType.DMA((2,)),
                pltpu.SemaphoreType.DMA((2,)),
                pltpu.SemaphoreType.DMA((cols - 1,)),
                pltpu.SemaphoreType.DMA((cols - 1,)),
                pltpu.SemaphoreType.DMA((cols,)),
                pltpu.SemaphoreType.DMA((cols,)),
            ],
            compiler_params=pltpu.CompilerParams(
                collective_id=0, has_side_effects=True, vmem_limit_bytes=32 << 20),
        )(psi0, onsite, hop_x, hop_y, cos_coef.T, sin_coef.T)

    placed = (P("col", "slab", None), P("slab", None), P("slab", None), P("slab", None), P(), P())
    return jax.shard_map(
        on_device,
        mesh=mesh,
        in_specs=placed,
        out_specs=P(None, None, "slab", "col"),
        check_vma=False,
    )
```

```python
import functools

import jax
import jax.numpy as jnp
from jax import lax
from jax.experimental import pallas as pl
from jax.experimental.pallas import tpu as pltpu
from jax.sharding import PartitionSpec as P

MESH = pl.DeviceIdType.MESH
CHUNKS = 8
LANES = 128


def kernel(slabs, cols, psi, onsite_hbm, hop_x_hbm, hop_y_hbm, cos_hbm, sin_hbm, out,
           onsite, hop_x, hop_y, cos_ref, sin_ref, input_sem, field, to_up, to_down, from_down, from_up, coef, states, first, second, beside, acc, part, extra,
           got, got_extra, local_sem, send_sem, recv_sem, coef_send, coef_recv,
           part_send, part_recv, extra_send, extra_recv):
    slab = lax.axis_index("slab")
    col = lax.axis_index("col")
    batch, rows, width = psi.shape
    per = batch // CHUNKS
    quarter = width // cols
    has_down = slab > 0
    has_up = slab < slabs - 1

    def span(i):
        return pl.ds(i * per, per)

    def local(i):
        return pltpu.make_async_copy(
            psi.at[span(i)], field.at[span(i), 2:6, :], local_sem.at[i])

    def upward(i):
        return pltpu.make_async_remote_copy(
            src_ref=psi.at[span(i), 2:4, :], dst_ref=field.at[span(i), 0:2, :],
            send_sem=send_sem.at[0, i], recv_sem=recv_sem.at[0, i],
            device_id=(slab + 1, col), device_id_type=MESH)

    def downward(i):
        return pltpu.make_async_remote_copy(
            src_ref=psi.at[span(i), 0:2, :], dst_ref=field.at[span(i), 6:8, :],
            send_sem=send_sem.at[1, i], recv_sem=recv_sem.at[1, i],
            device_id=(slab - 1, col), device_id_type=MESH)

    coef_up = pltpu.make_async_remote_copy(
        src_ref=to_up, dst_ref=from_down, send_sem=coef_send.at[0],
        recv_sem=coef_recv.at[0], device_id=(slab + 1, col), device_id_type=MESH)
    coef_down = pltpu.make_async_remote_copy(
        src_ref=to_down, dst_ref=from_up, send_sem=coef_send.at[1],
        recv_sem=coef_recv.at[1], device_id=(slab - 1, col), device_id_type=MESH)

    loads = [
        pltpu.make_async_copy(source, target, input_sem.at[n])
        for n, (source, target) in enumerate((
            (hop_x_hbm, hop_x), (onsite_hbm, onsite), (hop_y_hbm, hop_y),
            (cos_hbm, cos_ref), (sin_hbm, sin_ref)))]
    for load in loads:
        load.start()
    for i in range(CHUNKS):
        local(i).start()

    barrier = pltpu.get_barrier_semaphore()
    for by in range(1, cols):
        pl.semaphore_signal(barrier, inc=1, device_id=(slab, lax.rem(col + by, cols)),
                            device_id_type=MESH)

    @pl.when(has_up)
    def _():
        for other in range(cols):
            pl.semaphore_signal(barrier, inc=1, device_id=(slab + 1, other), device_id_type=MESH)

    @pl.when(has_down)
    def _():
        for other in range(cols):
            pl.semaphore_signal(barrier, inc=1, device_id=(slab - 1, other), device_id_type=MESH)

    for load in loads:
        load.wait()
    zero = jnp.zeros((1, width), jnp.float32)
    to_up[...] = jnp.concatenate(
        [hop_x[2:4, :], onsite[3:4, :], hop_y[3:4, :]], axis=0)
    to_down[...] = jnp.concatenate(
        [hop_x[0:1, :], onsite[0:1, :], hop_y[0:1, :], zero], axis=0)

    sides = jnp.where(has_up, 1, 0) + jnp.where(has_down, 1, 0)
    pl.semaphore_wait(barrier, cols - 1 + cols * sides)

    @pl.when(has_up)
    def _():
        coef_up.start()

    @pl.when(has_down)
    def _():
        coef_down.start()

    for i in range(CHUNKS):
        @pl.when(has_up)
        def _():
            upward(i).start()

        @pl.when(has_down)
        def _():
            downward(i).start()

    blank = jnp.zeros((batch, 2, width), jnp.bfloat16)

    @pl.when(jnp.logical_not(has_down))
    def _():
        field[:, 0:2, :] = blank
        from_down[...] = jnp.zeros_like(from_down)

    @pl.when(jnp.logical_not(has_up))
    def _():
        field[:, 6:8, :] = blank
        from_up[...] = jnp.zeros_like(from_up)

    acc[...] = jnp.zeros_like(acc)

    @pl.when(has_down)
    def _():
        coef_up.wait_recv()

    @pl.when(has_up)
    def _():
        coef_down.wait_recv()

    low = from_down[...]
    high = from_up[...]
    site_x = jnp.concatenate([low[0:2], hop_x[...], high[0:1], zero], axis=0)
    site_on = jnp.concatenate([zero, low[2:3], onsite[...], high[1:2], zero], axis=0)
    site_y = jnp.concatenate([zero, low[3:4], hop_y[...], high[2:3], zero], axis=0)
    row_id = lax.broadcasted_iota(jnp.int32, (8, width), 0)
    lane_id = lax.broadcasted_iota(jnp.int32, (8, width), 1)
    site_x = jnp.where((row_id == 5) & jnp.logical_not(has_up), 0.0, site_x)
    bond_y = jnp.where((lax.rem(row_id + lane_id, 2) == 0) & (lane_id < width - 1), site_y, 0.0)
    both_y = bond_y + pltpu.roll(bond_y, 1, 1)
    for x in range(8):
        coef[0, x] = jnp.broadcast_to(site_on[x:x + 1], (8, width))
        coef[1, x] = jnp.broadcast_to(site_x[x:x + 1], (8, width))
        coef[2, x] = jnp.broadcast_to(both_y[x:x + 1], (8, width))

    lane = lax.broadcasted_iota(jnp.int32, (8, LANES), 1)
    odd_lane = lax.rem(lane, 2)
    near = (lane + 1 - 2 * odd_lane, lax.rem(lane + LANES - 1 + 2 * odd_lane, LANES))
    first_lane = lane == 0
    last_lane = lane == LANES - 1
    even_lane = odd_lane == 0
    tiles = width // LANES

    def partner(f, x):
        parts = [
            jnp.take_along_axis(f[:, k * LANES:(k + 1) * LANES], near[x % 2], axis=1)
            for k in range(tiles)]
        if x % 2:
            parts = [
                jnp.where(last_lane, parts[(k + 1) % tiles],
                          jnp.where(first_lane, parts[k - 1], parts[k]))
                for k in range(tiles)]
        return jnp.concatenate(parts, axis=1)

    def rounded(f):
        return f.astype(jnp.bfloat16).astype(jnp.float32)

    def mixed(f, g):
        return jnp.concatenate([
            jnp.where(even_lane, f[:, k * LANES:(k + 1) * LANES], g[:, k * LANES:(k + 1) * LANES])
            for k in range(tiles)], axis=1)

    def p_row(x):
        return jnp.concatenate(
            [states[k, pl.ds(x + 2, 8, stride=8), :] for k in range(tiles)], axis=1)

    def hamiltonian(row, x, side):
        return (coef[0, x + 2] * row(x) - coef[1, x + 1] * row(x - 1)
                - coef[1, x + 2] * row(x + 1) - coef[2, x + 2] * side)

    def q_row(x):
        return first[x + 1]

    def t_row(x):
        return second[x]

    def chunk(i, carry):
        local(i).wait()

        @pl.when(has_down)
        def _():
            upward(i).wait_recv()

        @pl.when(has_up)
        def _():
            downward(i).wait_recv()

        def group(j, inner):
            for c in range(8):
                block = field[i * per + j * 8 + c].astype(jnp.float32)
                for k in range(tiles):
                    states[k, 8 * c:8 * c + 8, :] = block[:, k * LANES:(k + 1) * LANES]
            for x in range(-1, rows + 1):
                side = partner(p_row(x), x)
                if 0 <= x < rows:
                    beside[0, x] = side
                first[x + 1] = rounded(hamiltonian(p_row, x, side))
            for x in range(rows):
                side = partner(q_row(x), x)
                beside[1, x] = side
                t = rounded(2.0 * hamiltonian(q_row, x, side) - p_row(x))
                second[x] = t
                beside[2, x] = partner(t, x)
            for x in range(rows):
                acc[x] += p_row(x) * q_row(x + 1) - q_row(x) * p_row(x + 1)
                if x < rows - 1:
                    acc[8 + x] += p_row(x) * t_row(x + 1) - t_row(x) * p_row(x + 1)
                    acc[16 + x] += q_row(x) * t_row(x + 1) - t_row(x) * q_row(x + 1)
                else:
                    acc[8 + x] -= t_row(x) * p_row(x + 1)
                    acc[16 + x] -= t_row(x) * q_row(x + 1)
            acc[14] += p_row(-1) * t_row(0)
            acc[22] += q_row(-1) * t_row(0)
            for h in range(rows // 2):
                x = 2 * h
                own = (mixed(p_row(x), p_row(x + 1)), mixed(q_row(x), q_row(x + 1)),
                       mixed(t_row(x), t_row(x + 1)))
                side = [mixed(beside[n, x], beside[n, x + 1]) for n in range(3)]
                acc[4 + h] += own[0] * side[1] - own[1] * side[0]
                acc[12 + h] += own[0] * side[2] - own[2] * side[0]
                acc[20 + h] += own[1] * side[2] - own[2] * side[1]
            return inner

        return lax.fori_loop(0, per // 8, group, carry)

    lax.fori_loop(0, CHUNKS, chunk, 0)

    def folded(maps):
        size = 4
        while size:
            upper = lax.rem(row_id // size, 2) == 1
            half = len(maps) // 2
            maps = [
                jnp.where(upper, maps[n + half] + pltpu.roll(maps[n + half], size, 0),
                          maps[n] + pltpu.roll(maps[n], 8 - size, 0))
                for n in range(half)]
            size //= 2
        return maps[0]

    whole = [folded([acc[8 * k + n] for n in range(8)]) for k in range(3)]
    for k in range(3):
        for j in range(cols):
            part[j, k] = whole[k][:, j * quarter:(j + 1) * quarter]
    two = jnp.concatenate([whole[1][6:7], whole[2][6:7]], axis=0)
    for j in range(cols):
        extra[j] = two[:, j * quarter:(j + 1) * quarter]

    def to_peer(by):
        peer = lax.rem(col + by, cols)
        return pltpu.make_async_remote_copy(
            src_ref=part.at[peer], dst_ref=got.at[by - 1], send_sem=part_send.at[by - 1],
            recv_sem=part_recv.at[by - 1], device_id=(slab, peer), device_id_type=MESH)

    def to_below(by):
        peer = lax.rem(col + by, cols)
        return pltpu.make_async_remote_copy(
            src_ref=extra.at[peer], dst_ref=got_extra.at[by], send_sem=extra_send.at[by],
            recv_sem=extra_recv.at[by], device_id=(slab - 1, peer), device_id_type=MESH)

    for by in range(1, cols):
        to_peer(by).start()

    @pl.when(has_down)
    def _():
        for by in range(cols):
            to_below(by).start()

    @pl.when(jnp.logical_not(has_up))
    def _():
        got_extra[...] = jnp.zeros_like(got_extra)

    for by in range(1, cols):
        to_peer(by).wait_recv()

    @pl.when(has_up)
    def _():
        for by in range(cols):
            to_below(by).wait_recv()

    here = pl.ds(pl.multiple_of(col * quarter, quarter), quarter)
    extra_sum = got_extra[0] + got_extra[1] + got_extra[2] + got_extra[3]
    own_x = hop_x[:, here]
    own_y = hop_y[:, here]
    row4 = lax.broadcasted_iota(jnp.int32, (4, quarter), 0)
    lane4 = lax.broadcasted_iota(jnp.int32, (4, quarter), 1)
    keep = (lax.rem(row4 + lane4, 2) == 0) & (lane4 + col * quarter < width - 1)
    own_y = jnp.where(keep, own_y, 0.0)
    along = []
    across = []
    for k in range(3):
        total = part[col, k] + got[0, k] + got[1, k] + got[2, k]
        a = total[0:4]
        if k:
            a = a + jnp.where(row4 == 3, extra_sum[k - 1:k], 0.0)
        along.append(a * own_x)
        across.append(jnp.concatenate([total[4:5], total[4:5], total[5:6], total[5:6]], axis=0) * own_y)
    for e in range(cos_ref.shape[1]):
        c0, c1, c2 = (cos_ref[n, e] for n in range(3))
        s0, s1, s2 = (sin_ref[n, e] for n in range(3))
        d = (c0 * s1 - c1 * s0, c0 * s2 - c2 * s0, c1 * s2 - c2 * s1)
        out[e, 0] = d[0] * along[0] + d[1] * along[1] + d[2] * along[2]
        out[e, 1] = d[0] * across[0] + d[1] * across[1] + d[2] * across[2]

    @pl.when(has_up)
    def _():
        coef_up.wait_send()
        for i in range(CHUNKS):
            upward(i).wait_send()

    @pl.when(has_down)
    def _():
        coef_down.wait_send()
        for i in range(CHUNKS):
            downward(i).wait_send()
        for by in range(cols):
            to_below(by).wait_send()

    for by in range(1, cols):
        to_peer(by).wait_send()


def solution(mesh):
    slabs, cols = mesh.shape["slab"], mesh.shape["col"]

    def on_device(psi0, onsite, hop_x, hop_y, cos_coef, sin_coef):
        batch, rows, width = psi0.shape
        quarter = width // cols
        vmem = pl.BlockSpec(memory_space=pltpu.VMEM)
        hbm = pl.BlockSpec(memory_space=pltpu.HBM)
        f32 = jnp.float32
        return pl.pallas_call(
            functools.partial(kernel, slabs, cols),
            out_shape=jax.ShapeDtypeStruct((cos_coef.shape[0], 2, rows, quarter), f32),
            in_specs=[hbm] * 6,
            out_specs=vmem,
            scratch_shapes=[
                pltpu.VMEM((rows, width), f32),
                pltpu.VMEM((rows, width), f32),
                pltpu.VMEM((rows, width), f32),
                pltpu.SMEM(cos_coef.shape[::-1], f32),
                pltpu.SMEM(sin_coef.shape[::-1], f32),
                pltpu.SemaphoreType.DMA((5,)),
                pltpu.VMEM((batch, 8, width), jnp.bfloat16),
                pltpu.VMEM((4, width), f32),
                pltpu.VMEM((4, width), f32),
                pltpu.VMEM((4, width), f32),
                pltpu.VMEM((4, width), f32),
                pltpu.VMEM((3, 8, 8, width), f32),
                pltpu.VMEM((width // LANES, 64, LANES), f32),
                pltpu.VMEM((rows + 2, 8, width), f32),
                pltpu.VMEM((rows, 8, width), f32),
                pltpu.VMEM((3, rows, 8, width), f32),
                pltpu.VMEM((24, 8, width), f32),
                pltpu.VMEM((cols, 3, 8, quarter), f32),
                pltpu.VMEM((cols, 2, quarter), f32),
                pltpu.VMEM((cols - 1, 3, 8, quarter), f32),
                pltpu.VMEM((cols, 2, quarter), f32),
                pltpu.SemaphoreType.DMA((CHUNKS,)),
                pltpu.SemaphoreType.DMA((2, CHUNKS)),
                pltpu.SemaphoreType.DMA((2, CHUNKS)),
                pltpu.SemaphoreType.DMA((2,)),
                pltpu.SemaphoreType.DMA((2,)),
                pltpu.SemaphoreType.DMA((cols - 1,)),
                pltpu.SemaphoreType.DMA((cols - 1,)),
                pltpu.SemaphoreType.DMA((cols,)),
                pltpu.SemaphoreType.DMA((cols,)),
            ],
            compiler_params=pltpu.CompilerParams(
                collective_id=0, has_side_effects=True, vmem_limit_bytes=60 << 20),
        )(psi0, onsite, hop_x, hop_y, cos_coef.T, sin_coef.T)

    placed = (P("col", "slab", None), P("slab", None), P("slab", None), P("slab", None), P(), P())
    return jax.shard_map(
        on_device,
        mesh=mesh,
        in_specs=placed,
        out_specs=P(None, None, "slab", "col"),
        check_vma=False,
    )
```

```python
import functools

import jax
import jax.numpy as jnp
from jax import lax
from jax.experimental import pallas as pl
from jax.experimental.pallas import tpu as pltpu
from jax.sharding import PartitionSpec as P

MESH = pl.DeviceIdType.MESH
CHUNKS = 8
LANES = 128
AHEAD = 2


def kernel(slabs, cols, psi, onsite_hbm, hop_x_hbm, hop_y_hbm, cos_hbm, sin_hbm, out,
           onsite, hop_x, hop_y, cos_ref, sin_ref, input_sem, field, to_up, to_down, from_down, from_up, coef, states, first, second, beside, acc, part, extra,
           got, got_extra, local_sem, send_sem, recv_sem, coef_send, coef_recv,
           part_send, part_recv, extra_send, extra_recv, go):
    slab = lax.axis_index("slab")
    col = lax.axis_index("col")
    batch, rows, width = psi.shape
    per = batch // CHUNKS
    quarter = width // cols
    has_down = slab > 0
    has_up = slab < slabs - 1

    def span(i):
        return pl.ds(i * per, per)

    def local(i):
        return pltpu.make_async_copy(
            psi.at[span(i)], field.at[span(i), 2:6, :], local_sem.at[i])

    def upward(i):
        return pltpu.make_async_remote_copy(
            src_ref=psi.at[span(i), 2:4, :], dst_ref=field.at[span(i), 0:2, :],
            send_sem=send_sem.at[0, i], recv_sem=recv_sem.at[0, i],
            device_id=(slab + 1, col), device_id_type=MESH)

    def downward(i):
        return pltpu.make_async_remote_copy(
            src_ref=psi.at[span(i), 0:2, :], dst_ref=field.at[span(i), 6:8, :],
            send_sem=send_sem.at[1, i], recv_sem=recv_sem.at[1, i],
            device_id=(slab - 1, col), device_id_type=MESH)

    coef_up = pltpu.make_async_remote_copy(
        src_ref=to_up, dst_ref=from_down, send_sem=coef_send.at[0],
        recv_sem=coef_recv.at[0], device_id=(slab + 1, col), device_id_type=MESH)
    coef_down = pltpu.make_async_remote_copy(
        src_ref=to_down, dst_ref=from_up, send_sem=coef_send.at[1],
        recv_sem=coef_recv.at[1], device_id=(slab - 1, col), device_id_type=MESH)

    place = lax.rem(slab, 4)
    is_0, is_1, is_2, is_3 = (place == n for n in range(4))

    def greet(sem_of, other):
        for by in range(cols):
            pl.semaphore_signal(sem_of, inc=1, device_id=(other, lax.rem(col + by, cols)),
                                device_id_type=MESH)

    barrier = pltpu.get_barrier_semaphore()

    @pl.when((is_0 | is_1) & has_up)
    def _():
        greet(barrier, slab + 1)

    @pl.when(jnp.logical_not(is_2) & has_down)
    def _():
        greet(barrier, slab - 1)

    @pl.when(jnp.logical_not(is_3))
    def _():
        for by in range(1, cols):
            pl.semaphore_signal(barrier, inc=1, device_id=(slab, lax.rem(col + by, cols)),
                                device_id_type=MESH)

    @pl.when(jnp.logical_not(is_3) | has_up)
    def _():
        pl.semaphore_wait(barrier, jnp.where(
            is_3, cols, jnp.where(is_2, 3 * cols - 1, 2 * cols - 1)))

    def send_up(chunks):
        for i in chunks:
            upward(i).start()

    def send_down(chunks):
        for i in chunks:
            downward(i).start()

    ready_up = jnp.logical_not(is_1) & has_up
    ready_down = (is_1 | is_2) & has_down
    asked_up = is_1 & has_up
    asked_down = (is_0 | is_3) & has_down
    asked = asked_up | asked_down

    @pl.when(ready_up)
    def _():
        send_up(range(AHEAD))

    @pl.when(ready_down)
    def _():
        send_down(range(AHEAD))

    @pl.when(is_2 | (is_3 & has_up))
    def _():
        for by in range(cols):
            pl.semaphore_signal(go.at[col], inc=1, device_id=(slab + 1, lax.rem(col + by, cols)),
                                device_id_type=MESH)

    @pl.when(is_2)
    def _():
        for by in range(cols):
            pl.semaphore_signal(go.at[col], inc=1, device_id=(slab - 1, lax.rem(col + by, cols)),
                                device_id_type=MESH)

    loads = [
        pltpu.make_async_copy(source, target, input_sem.at[n])
        for n, (source, target) in enumerate((
            (hop_x_hbm, hop_x), (onsite_hbm, onsite), (hop_y_hbm, hop_y),
            (cos_hbm, cos_ref), (sin_hbm, sin_ref)))]
    for load in loads:
        load.start()
    for load in loads:
        load.wait()
    zero = jnp.zeros((1, width), jnp.float32)
    to_up[...] = jnp.concatenate(
        [hop_x[2:4, :], onsite[3:4, :], hop_y[3:4, :]], axis=0)
    to_down[...] = jnp.concatenate(
        [hop_x[0:1, :], onsite[0:1, :], hop_y[0:1, :], zero], axis=0)

    @pl.when(ready_up)
    def _():
        coef_up.start()
        send_up(range(AHEAD, CHUNKS))

    @pl.when(ready_down)
    def _():
        coef_down.start()
        send_down(range(AHEAD, CHUNKS))

    for i in range(CHUNKS):
        local(i).start()


    blank = jnp.zeros((batch, 2, width), jnp.bfloat16)

    @pl.when(jnp.logical_not(has_down))
    def _():
        field[:, 0:2, :] = blank
        from_down[...] = jnp.zeros_like(from_down)

    @pl.when(jnp.logical_not(has_up))
    def _():
        field[:, 6:8, :] = blank
        from_up[...] = jnp.zeros_like(from_up)

    acc[...] = jnp.zeros_like(acc)

    @pl.when(asked)
    def _():
        pl.semaphore_wait(go.at[col], 1)

    @pl.when(asked_up)
    def _():
        send_up(range(AHEAD))
        coef_up.start()
        send_up(range(AHEAD, CHUNKS))

    @pl.when(asked_down)
    def _():
        send_down(range(AHEAD))
        coef_down.start()
        send_down(range(AHEAD, CHUNKS))

    @pl.when(has_down)
    def _():
        coef_up.wait_recv()

    @pl.when(has_up)
    def _():
        coef_down.wait_recv()

    low = from_down[...]
    high = from_up[...]
    site_x = jnp.concatenate([low[0:2], hop_x[...], high[0:1], zero], axis=0)
    site_on = jnp.concatenate([zero, low[2:3], onsite[...], high[1:2], zero], axis=0)
    site_y = jnp.concatenate([zero, low[3:4], hop_y[...], high[2:3], zero], axis=0)
    row_id = lax.broadcasted_iota(jnp.int32, (8, width), 0)
    lane_id = lax.broadcasted_iota(jnp.int32, (8, width), 1)
    site_x = jnp.where((row_id == 5) & jnp.logical_not(has_up), 0.0, site_x)
    bond_y = jnp.where((lax.rem(row_id + lane_id, 2) == 0) & (lane_id < width - 1), site_y, 0.0)
    both_y = bond_y + pltpu.roll(bond_y, 1, 1)
    for x in range(8):
        coef[0, x] = jnp.broadcast_to(site_on[x:x + 1], (8, width))
        coef[1, x] = jnp.broadcast_to(site_x[x:x + 1], (8, width))
        coef[2, x] = jnp.broadcast_to(both_y[x:x + 1], (8, width))

    lane = lax.broadcasted_iota(jnp.int32, (8, LANES), 1)
    odd_lane = lax.rem(lane, 2)
    near = (lane + 1 - 2 * odd_lane, lax.rem(lane + LANES - 1 + 2 * odd_lane, LANES))
    first_lane = lane == 0
    last_lane = lane == LANES - 1
    even_lane = odd_lane == 0
    tiles = width // LANES

    def partner(f, x):
        parts = [
            jnp.take_along_axis(f[:, k * LANES:(k + 1) * LANES], near[x % 2], axis=1)
            for k in range(tiles)]
        if x % 2:
            parts = [
                jnp.where(last_lane, parts[(k + 1) % tiles],
                          jnp.where(first_lane, parts[k - 1], parts[k]))
                for k in range(tiles)]
        return jnp.concatenate(parts, axis=1)

    def rounded(f):
        return f.astype(jnp.bfloat16).astype(jnp.float32)

    def mixed(f, g):
        return jnp.concatenate([
            jnp.where(even_lane, f[:, k * LANES:(k + 1) * LANES], g[:, k * LANES:(k + 1) * LANES])
            for k in range(tiles)], axis=1)

    def p_row(x):
        return jnp.concatenate(
            [states[k, pl.ds(x + 2, 8, stride=8), :] for k in range(tiles)], axis=1)

    def hamiltonian(row, x, side):
        return (coef[0, x + 2] * row(x) - coef[1, x + 1] * row(x - 1)
                - coef[1, x + 2] * row(x + 1) - coef[2, x + 2] * side)

    def q_row(x):
        return first[x + 1]

    def t_row(x):
        return second[x]

    def chunk(i, carry):
        local(i).wait()

        @pl.when(has_down)
        def _():
            upward(i).wait_recv()

        @pl.when(has_up)
        def _():
            downward(i).wait_recv()

        def group(j, inner):
            for c in range(8):
                block = field[i * per + j * 8 + c].astype(jnp.float32)
                for k in range(tiles):
                    states[k, 8 * c:8 * c + 8, :] = block[:, k * LANES:(k + 1) * LANES]
            for x in range(-1, rows + 1):
                side = partner(p_row(x), x)
                if 0 <= x < rows:
                    beside[0, x] = side
                first[x + 1] = rounded(hamiltonian(p_row, x, side))
            for x in range(rows):
                side = partner(q_row(x), x)
                beside[1, x] = side
                t = rounded(2.0 * hamiltonian(q_row, x, side) - p_row(x))
                second[x] = t
                beside[2, x] = partner(t, x)
            for x in range(rows):
                acc[x] += p_row(x) * q_row(x + 1) - q_row(x) * p_row(x + 1)
                if x < rows - 1:
                    acc[8 + x] += p_row(x) * t_row(x + 1) - t_row(x) * p_row(x + 1)
                    acc[16 + x] += q_row(x) * t_row(x + 1) - t_row(x) * q_row(x + 1)
                else:
                    acc[8 + x] -= t_row(x) * p_row(x + 1)
                    acc[16 + x] -= t_row(x) * q_row(x + 1)
            acc[14] += p_row(-1) * t_row(0)
            acc[22] += q_row(-1) * t_row(0)
            for h in range(rows // 2):
                x = 2 * h
                own = (mixed(p_row(x), p_row(x + 1)), mixed(q_row(x), q_row(x + 1)),
                       mixed(t_row(x), t_row(x + 1)))
                side = [mixed(beside[n, x], beside[n, x + 1]) for n in range(3)]
                acc[4 + h] += own[0] * side[1] - own[1] * side[0]
                acc[12 + h] += own[0] * side[2] - own[2] * side[0]
                acc[20 + h] += own[1] * side[2] - own[2] * side[1]
            return inner

        return lax.fori_loop(0, per // 8, group, carry)

    lax.fori_loop(0, CHUNKS, chunk, 0)

    @pl.when(asked)
    def _():
        for by in range(1, cols):
            pl.semaphore_wait(go.at[lax.rem(col + by, cols)], 1)

    fold_row = lax.broadcasted_iota(jnp.int32, (8, quarter), 0)

    def folded(maps):
        size = 4
        while size:
            upper = lax.rem(fold_row // size, 2) == 1
            half = len(maps) // 2
            maps = [
                jnp.where(upper, maps[n + half] + pltpu.roll(maps[n + half], size, 0),
                          maps[n] + pltpu.roll(maps[n], 8 - size, 0))
                for n in range(half)]
            size //= 2
        return maps[0]

    def to_peer(by):
        return pltpu.make_async_remote_copy(
            src_ref=part.at[by], dst_ref=got.at[by - 1], send_sem=part_send.at[by - 1],
            recv_sem=part_recv.at[by - 1], device_id=(slab, lax.rem(col + by, cols)),
            device_id_type=MESH)

    def to_below(by):
        return pltpu.make_async_remote_copy(
            src_ref=extra.at[by], dst_ref=got_extra.at[by], send_sem=extra_send.at[by],
            recv_sem=extra_recv.at[by], device_id=(slab - 1, lax.rem(col + by, cols)),
            device_id_type=MESH)

    for by in (2, 1, 3, 0):
        there = pl.ds(pl.multiple_of(lax.rem(col + by, cols) * quarter, quarter), quarter)
        for k in range(3):
            whole = folded([acc[8 * k + n, :, there] for n in range(8)])
            part[by, k] = whole
            if k:
                extra[by, k - 1:k] = whole[6:7]
        if by:
            to_peer(by).start()

        @pl.when(has_down)
        def _():
            to_below(by).start()

    @pl.when(jnp.logical_not(has_up))
    def _():
        got_extra[...] = jnp.zeros_like(got_extra)

    for by in range(1, cols):
        to_peer(by).wait_recv()

    @pl.when(has_up)
    def _():
        for by in range(cols):
            to_below(by).wait_recv()

    here = pl.ds(pl.multiple_of(col * quarter, quarter), quarter)
    extra_sum = got_extra[0] + got_extra[1] + got_extra[2] + got_extra[3]
    own_x = hop_x[:, here]
    own_y = hop_y[:, here]
    row4 = lax.broadcasted_iota(jnp.int32, (4, quarter), 0)
    lane4 = lax.broadcasted_iota(jnp.int32, (4, quarter), 1)
    keep = (lax.rem(row4 + lane4, 2) == 0) & (lane4 + col * quarter < width - 1)
    own_y = jnp.where(keep, own_y, 0.0)
    along = []
    across = []
    for k in range(3):
        total = part[0, k] + got[0, k] + got[1, k] + got[2, k]
        a = total[0:4]
        if k:
            a = a + jnp.where(row4 == 3, extra_sum[k - 1:k], 0.0)
        along.append(a * own_x)
        across.append(jnp.concatenate([total[4:5], total[4:5], total[5:6], total[5:6]], axis=0) * own_y)
    for e in range(cos_ref.shape[1]):
        c0, c1, c2 = (cos_ref[n, e] for n in range(3))
        s0, s1, s2 = (sin_ref[n, e] for n in range(3))
        d = (c0 * s1 - c1 * s0, c0 * s2 - c2 * s0, c1 * s2 - c2 * s1)
        out[e, 0] = d[0] * along[0] + d[1] * along[1] + d[2] * along[2]
        out[e, 1] = d[0] * across[0] + d[1] * across[1] + d[2] * across[2]

    @pl.when(has_up)
    def _():
        coef_up.wait_send()
        for i in range(CHUNKS):
            upward(i).wait_send()

    @pl.when(has_down)
    def _():
        coef_down.wait_send()
        for i in range(CHUNKS):
            downward(i).wait_send()
        for by in range(cols):
            to_below(by).wait_send()

    for by in range(1, cols):
        to_peer(by).wait_send()


def solution(mesh):
    slabs, cols = mesh.shape["slab"], mesh.shape["col"]

    def on_device(psi0, onsite, hop_x, hop_y, cos_coef, sin_coef):
        batch, rows, width = psi0.shape
        quarter = width // cols
        vmem = pl.BlockSpec(memory_space=pltpu.VMEM)
        hbm = pl.BlockSpec(memory_space=pltpu.HBM)
        f32 = jnp.float32
        return pl.pallas_call(
            functools.partial(kernel, slabs, cols),
            out_shape=jax.ShapeDtypeStruct((cos_coef.shape[0], 2, rows, quarter), f32),
            in_specs=[hbm] * 6,
            out_specs=vmem,
            scratch_shapes=[
                pltpu.VMEM((rows, width), f32),
                pltpu.VMEM((rows, width), f32),
                pltpu.VMEM((rows, width), f32),
                pltpu.SMEM(cos_coef.shape[::-1], f32),
                pltpu.SMEM(sin_coef.shape[::-1], f32),
                pltpu.SemaphoreType.DMA((5,)),
                pltpu.VMEM((batch, 8, width), jnp.bfloat16),
                pltpu.VMEM((4, width), f32),
                pltpu.VMEM((4, width), f32),
                pltpu.VMEM((4, width), f32),
                pltpu.VMEM((4, width), f32),
                pltpu.VMEM((3, 8, 8, width), f32),
                pltpu.VMEM((width // LANES, 64, LANES), f32),
                pltpu.VMEM((rows + 2, 8, width), f32),
                pltpu.VMEM((rows, 8, width), f32),
                pltpu.VMEM((3, rows, 8, width), f32),
                pltpu.VMEM((24, 8, width), f32),
                pltpu.VMEM((cols, 3, 8, quarter), f32),
                pltpu.VMEM((cols, 2, quarter), f32),
                pltpu.VMEM((cols - 1, 3, 8, quarter), f32),
                pltpu.VMEM((cols, 2, quarter), f32),
                pltpu.SemaphoreType.DMA((CHUNKS,)),
                pltpu.SemaphoreType.DMA((2, CHUNKS)),
                pltpu.SemaphoreType.DMA((2, CHUNKS)),
                pltpu.SemaphoreType.DMA((2,)),
                pltpu.SemaphoreType.DMA((2,)),
                pltpu.SemaphoreType.DMA((cols - 1,)),
                pltpu.SemaphoreType.DMA((cols - 1,)),
                pltpu.SemaphoreType.DMA((cols,)),
                pltpu.SemaphoreType.DMA((cols,)),
                pltpu.SemaphoreType.REGULAR((cols,)),
            ],
            compiler_params=pltpu.CompilerParams(
                collective_id=0, has_side_effects=True, vmem_limit_bytes=32 << 20),
        )(*(pltpu.with_memory_space_constraint(a, pltpu.HBM) for a in (
            psi0, onsite, hop_x, hop_y, cos_coef.T, sin_coef.T)))

    placed = (P("col", "slab", None), P("slab", None), P("slab", None), P("slab", None), P(), P())
    return jax.shard_map(
        on_device,
        mesh=mesh,
        in_specs=placed,
        out_specs=P(None, None, "slab", "col"),
        check_vma=False,
    )
```

```python
import functools

import jax
import jax.numpy as jnp
from jax import lax
from jax.experimental import pallas as pl
from jax.experimental.pallas import tpu as pltpu
from jax.sharding import PartitionSpec as P

MESH = pl.DeviceIdType.MESH
CHUNKS = 8
LANES = 128
AHEAD = 2


def kernel(slabs, cols, psi, onsite_hbm, hop_x_hbm, hop_y_hbm, cos_hbm, sin_hbm, out,
           onsite, hop_x, hop_y, cos_ref, sin_ref, input_sem, field, to_up, to_down, from_down, from_up, coef, states, first, second, beside, acc, sums, kept, part, extra,
           got, got_extra, local_sem, send_sem, recv_sem, coef_send, coef_recv,
           part_send, part_recv, extra_send, extra_recv, go):
    slab = lax.axis_index("slab")
    col = lax.axis_index("col")
    batch, rows, width = psi.shape
    per = batch // CHUNKS
    quarter = width // cols
    has_down = slab > 0
    has_up = slab < slabs - 1

    def span(i):
        return pl.ds(i * per, per)

    def local(i):
        return pltpu.make_async_copy(
            psi.at[span(i)], field.at[span(i), 2:6, :], local_sem.at[i])

    def upward(i):
        return pltpu.make_async_remote_copy(
            src_ref=psi.at[span(i), 2:4, :], dst_ref=field.at[span(i), 0:2, :],
            send_sem=send_sem.at[0, i], recv_sem=recv_sem.at[0, i],
            device_id=(slab + 1, col), device_id_type=MESH)

    def downward(i):
        return pltpu.make_async_remote_copy(
            src_ref=psi.at[span(i), 0:2, :], dst_ref=field.at[span(i), 6:8, :],
            send_sem=send_sem.at[1, i], recv_sem=recv_sem.at[1, i],
            device_id=(slab - 1, col), device_id_type=MESH)

    coef_up = pltpu.make_async_remote_copy(
        src_ref=to_up, dst_ref=from_down, send_sem=coef_send.at[0],
        recv_sem=coef_recv.at[0], device_id=(slab + 1, col), device_id_type=MESH)
    coef_down = pltpu.make_async_remote_copy(
        src_ref=to_down, dst_ref=from_up, send_sem=coef_send.at[1],
        recv_sem=coef_recv.at[1], device_id=(slab - 1, col), device_id_type=MESH)

    place = lax.rem(slab, 4)
    is_0, is_1, is_2, is_3 = (place == n for n in range(4))

    def greet(sem_of, other):
        for by in range(cols):
            pl.semaphore_signal(sem_of, inc=1, device_id=(other, lax.rem(col + by, cols)),
                                device_id_type=MESH)

    barrier = pltpu.get_barrier_semaphore()

    @pl.when((is_0 | is_1) & has_up)
    def _():
        greet(barrier, slab + 1)

    @pl.when(jnp.logical_not(is_2) & has_down)
    def _():
        greet(barrier, slab - 1)

    @pl.when(is_2)
    def _():
        pl.semaphore_signal(barrier, inc=1, device_id=(slab - 1, col), device_id_type=MESH)

    @pl.when(jnp.logical_not(is_3))
    def _():
        for by in range(1, cols):
            pl.semaphore_signal(barrier, inc=1, device_id=(slab, lax.rem(col + by, cols)),
                                device_id_type=MESH)

    @pl.when(jnp.logical_not(is_3) | has_up)
    def _():
        pl.semaphore_wait(barrier, jnp.where(
            is_3, cols, jnp.where(is_2, 3 * cols - 1, jnp.where(is_1, 2 * cols, 2 * cols - 1))))

    def send_up(chunks):
        for i in chunks:
            upward(i).start()

    def send_down(chunks):
        for i in chunks:
            downward(i).start()

    ready_up = has_up
    ready_down = (is_1 | is_2) & has_down
    asked = (is_0 | is_3) & has_down

    @pl.when(ready_up)
    def _():
        send_up(range(AHEAD))

    @pl.when(ready_down)
    def _():
        send_down(range(AHEAD))

    @pl.when(is_2 | (is_3 & has_up))
    def _():
        for by in range(cols):
            pl.semaphore_signal(go.at[col], inc=1, device_id=(slab + 1, lax.rem(col + by, cols)),
                                device_id_type=MESH)

    loads = [
        pltpu.make_async_copy(source, target, input_sem.at[n])
        for n, (source, target) in enumerate((
            (hop_x_hbm, hop_x), (onsite_hbm, onsite), (hop_y_hbm, hop_y),
            (cos_hbm, cos_ref), (sin_hbm, sin_ref)))]
    for load in loads:
        load.start()
    for load in loads:
        load.wait()
    zero = jnp.zeros((1, width), jnp.float32)
    to_up[...] = jnp.concatenate(
        [hop_x[2:4, :], onsite[3:4, :], hop_y[3:4, :]], axis=0)
    to_down[...] = jnp.concatenate(
        [hop_x[0:1, :], onsite[0:1, :], hop_y[0:1, :], zero], axis=0)

    @pl.when(ready_up)
    def _():
        coef_up.start()
        send_up(range(AHEAD, CHUNKS))

    @pl.when(ready_down)
    def _():
        coef_down.start()
        send_down(range(AHEAD, CHUNKS))

    for i in range(CHUNKS):
        local(i).start()


    blank = jnp.zeros((batch, 2, width), jnp.bfloat16)

    @pl.when(jnp.logical_not(has_down))
    def _():
        field[:, 0:2, :] = blank
        from_down[...] = jnp.zeros_like(from_down)

    @pl.when(jnp.logical_not(has_up))
    def _():
        field[:, 6:8, :] = blank
        from_up[...] = jnp.zeros_like(from_up)

    acc[...] = jnp.zeros_like(acc)
    sums[...] = jnp.zeros_like(sums)

    @pl.when(asked)
    def _():
        pl.semaphore_wait(go.at[col], 1)
        send_down(range(AHEAD))
        coef_down.start()
        send_down(range(AHEAD, CHUNKS))

    @pl.when(has_down)
    def _():
        coef_up.wait_recv()

    @pl.when(has_up)
    def _():
        coef_down.wait_recv()

    low = from_down[...]
    high = from_up[...]
    site_x = jnp.concatenate([low[0:2], hop_x[...], high[0:1], zero], axis=0)
    site_on = jnp.concatenate([zero, low[2:3], onsite[...], high[1:2], zero], axis=0)
    site_y = jnp.concatenate([zero, low[3:4], hop_y[...], high[2:3], zero], axis=0)
    row_id = lax.broadcasted_iota(jnp.int32, (8, width), 0)
    lane_id = lax.broadcasted_iota(jnp.int32, (8, width), 1)
    site_x = jnp.where((row_id == 5) & jnp.logical_not(has_up), 0.0, site_x)
    bond_y = jnp.where((lax.rem(row_id + lane_id, 2) == 0) & (lane_id < width - 1), site_y, 0.0)
    both_y = bond_y + pltpu.roll(bond_y, 1, 1)
    for x in range(8):
        coef[0, x] = jnp.broadcast_to(site_on[x:x + 1], (8, width))
        coef[1, x] = jnp.broadcast_to(site_x[x:x + 1], (8, width))
        coef[2, x] = jnp.broadcast_to(both_y[x:x + 1], (8, width))

    lane = lax.broadcasted_iota(jnp.int32, (8, LANES), 1)
    odd_lane = lax.rem(lane, 2)
    near = (lane + 1 - 2 * odd_lane, lax.rem(lane + LANES - 1 + 2 * odd_lane, LANES))
    first_lane = lane == 0
    last_lane = lane == LANES - 1
    even_lane = odd_lane == 0
    tiles = width // LANES

    def partner(f, x):
        parts = [
            jnp.take_along_axis(f[:, k * LANES:(k + 1) * LANES], near[x % 2], axis=1)
            for k in range(tiles)]
        if x % 2:
            parts = [
                jnp.where(last_lane, parts[(k + 1) % tiles],
                          jnp.where(first_lane, parts[k - 1], parts[k]))
                for k in range(tiles)]
        return jnp.concatenate(parts, axis=1)

    def rounded(f):
        return f.astype(jnp.bfloat16).astype(jnp.float32)

    def load_states(g, count):
        for c in range(8):
            block = field[g * 8 + c, 0:count, :].astype(jnp.float32)
            for k in range(tiles):
                states[k, 8 * c:8 * c + count, :] = block[:, k * LANES:(k + 1) * LANES]

    def p_row(x):
        return jnp.concatenate(
            [states[k, pl.ds(x + 2, 8, stride=8), :] for k in range(tiles)], axis=1)

    def hamiltonian(row, x, side):
        return (coef[0, x + 2] * row(x) - coef[1, x + 1] * row(x - 1)
                - coef[1, x + 2] * row(x + 1) - coef[2, x + 2] * side)

    def lower(g):
        load_states(g, 6)
        for x in range(-1, 2):
            side = partner(p_row(x), x)
            q = rounded(hamiltonian(p_row, x, side))
            if x < 0:
                first[0] = q
            else:
                kept[g, x] = q
                kept[g, 3 + x] = side

        def q_row(x):
            return first[0] if x < 0 else kept[g, x]

        side = partner(q_row(0), 0)
        kept[g, 5] = side
        t = rounded(2.0 * hamiltonian(q_row, 0, side) - p_row(0))
        kept[g, 2] = t
        sums[0] += p_row(-1) * t
        sums[1] += q_row(-1) * t

    def upper(g):
        load_states(g, 8)

        def q_row(x):
            return kept[g, x] if x < 2 else first[x - 1]

        beside[0, 0] = kept[g, 3]
        beside[0, 1] = kept[g, 4]
        beside[1, 0] = kept[g, 5]
        second[0] = kept[g, 2]
        beside[2, 0] = partner(kept[g, 2], 0)
        for x in range(2, rows + 1):
            side = partner(p_row(x), x)
            if x < rows:
                beside[0, x] = side
            first[x - 1] = rounded(hamiltonian(p_row, x, side))
        for x in range(1, rows):
            side = partner(q_row(x), x)
            beside[1, x] = side
            t = rounded(2.0 * hamiltonian(q_row, x, side) - p_row(x))
            second[x] = t
            beside[2, x] = partner(t, x)

    def products(g, tile):
        lanes = pl.ds(pl.multiple_of(tile * LANES, LANES), LANES)

        def p(x):
            return states[tile, pl.ds(x + 2, 8, stride=8), :]

        def q(x):
            return kept[g, x, :, lanes] if x < 2 else first[x - 1, :, lanes]

        def t(x):
            return second[x, :, lanes]

        def add(n, value):
            acc[n, :, lanes] += value

        for x in range(rows):
            add(x, p(x) * q(x + 1) - q(x) * p(x + 1))
            if x < rows - 1:
                add(8 + x, p(x) * t(x + 1) - t(x) * p(x + 1))
                add(16 + x, q(x) * t(x + 1) - t(x) * q(x + 1))
            else:
                add(8 + x, -t(x) * p(x + 1))
                add(16 + x, -t(x) * q(x + 1))
        for h in range(rows // 2):
            x = 2 * h
            own = [jnp.where(even_lane, row(x), row(x + 1)) for row in (p, q, t)]
            side = [
                jnp.where(even_lane, beside[n, x, :, lanes], beside[n, x + 1, :, lanes])
                for n in range(3)]
            add(4 + h, own[0] * side[1] - own[1] * side[0])
            add(12 + h, own[0] * side[2] - own[2] * side[0])
            add(20 + h, own[1] * side[2] - own[2] * side[1])

    def to_peer(by):
        return pltpu.make_async_remote_copy(
            src_ref=part.at[by], dst_ref=got.at[by - 1], send_sem=part_send.at[by - 1],
            recv_sem=part_recv.at[by - 1], device_id=(slab, lax.rem(col + by, cols)),
            device_id_type=MESH)

    def to_below(by):
        peer = lax.rem(col + by, cols)
        return pltpu.make_async_remote_copy(
            src_ref=extra.at[peer], dst_ref=got_extra.at[by], send_sem=extra_send.at[by],
            recv_sem=extra_recv.at[by], device_id=(slab - 1, peer),
            device_id_type=MESH)

    def wait_lower(i):
        local(i).wait()

        @pl.when(has_down)
        def _():
            upward(i).wait_recv()

    def wait_upper(i):
        @pl.when(has_up)
        def _():
            downward(i).wait_recv()

    def send_extra():
        @pl.when(asked)
        def _():
            for by in range(1, cols):
                pl.semaphore_wait(go.at[lax.rem(col + by, cols)], 1)

        @pl.when(has_down)
        def _():
            for n in range(2):
                total = jnp.sum(sums[n], axis=0, keepdims=True)
                for j in range(cols):
                    extra[j, n:n + 1] = total[:, j * quarter:(j + 1) * quarter]
            for by in (2, 1, 3, 0):
                to_below(by).start()

    @pl.when(jnp.logical_not(is_0))
    def _():
        def lower_chunk(i, carry):
            wait_lower(i)
            lower(i)
            return carry

        lax.fori_loop(0, CHUNKS, lower_chunk, 0)
        send_extra()

    def chunk(i):
        @pl.when(is_0)
        def _():
            wait_lower(i)
            lower(i)

        wait_upper(i)
        upper(i)

    def whole_chunk(i, carry):
        chunk(i)
        for k in range(tiles):
            products(i, k)
        return carry

    lax.fori_loop(0, CHUNKS - 1, whole_chunk, 0)
    last = CHUNKS - 1
    chunk(last)

    fold_row = lax.broadcasted_iota(jnp.int32, (8, quarter), 0)

    def folded(maps):
        size = 4
        while size:
            upper_rows = lax.rem(fold_row // size, 2) == 1
            half = len(maps) // 2
            maps = [
                jnp.where(upper_rows, maps[n + half] + pltpu.roll(maps[n + half], size, 0),
                          maps[n] + pltpu.roll(maps[n], 8 - size, 0))
                for n in range(half)]
            size //= 2
        return maps[0]

    per_quarter = quarter // LANES
    for by in (2, 1, 3, 0):
        peer = lax.rem(col + by, cols)
        there = pl.ds(pl.multiple_of(peer * quarter, quarter), quarter)
        for k in range(per_quarter):
            products(last, peer * per_quarter + k)
        for k in range(3):
            maps = [acc[8 * k + n, :, there] for n in range(6)]
            part[by, k] = folded(maps + maps[4:6])
        if by:
            to_peer(by).start()

    @pl.when(is_0)
    def _():
        send_extra()

    @pl.when(jnp.logical_not(has_up))
    def _():
        got_extra[...] = jnp.zeros_like(got_extra)

    for by in range(1, cols):
        to_peer(by).wait_recv()

    @pl.when(has_up)
    def _():
        for by in range(cols):
            to_below(by).wait_recv()

    here = pl.ds(pl.multiple_of(col * quarter, quarter), quarter)
    extra_sum = got_extra[0] + got_extra[1] + got_extra[2] + got_extra[3]
    own_x = hop_x[:, here]
    own_y = hop_y[:, here]
    row4 = lax.broadcasted_iota(jnp.int32, (4, quarter), 0)
    lane4 = lax.broadcasted_iota(jnp.int32, (4, quarter), 1)
    keep = (lax.rem(row4 + lane4, 2) == 0) & (lane4 + col * quarter < width - 1)
    own_y = jnp.where(keep, own_y, 0.0)
    along = []
    across = []
    for k in range(3):
        total = part[0, k] + got[0, k] + got[1, k] + got[2, k]
        a = total[0:4]
        if k:
            a = a + jnp.where(row4 == 3, extra_sum[k - 1:k], 0.0)
        along.append(a * own_x)
        across.append(jnp.concatenate([total[4:5], total[4:5], total[5:6], total[5:6]], axis=0) * own_y)
    for e in range(cos_ref.shape[1]):
        c0, c1, c2 = (cos_ref[n, e] for n in range(3))
        s0, s1, s2 = (sin_ref[n, e] for n in range(3))
        d = (c0 * s1 - c1 * s0, c0 * s2 - c2 * s0, c1 * s2 - c2 * s1)
        out[e, 0] = d[0] * along[0] + d[1] * along[1] + d[2] * along[2]
        out[e, 1] = d[0] * across[0] + d[1] * across[1] + d[2] * across[2]

    @pl.when(has_up)
    def _():
        coef_up.wait_send()
        for i in range(CHUNKS):
            upward(i).wait_send()

    @pl.when(has_down)
    def _():
        coef_down.wait_send()
        for i in range(CHUNKS):
            downward(i).wait_send()
        for by in range(cols):
            to_below(by).wait_send()

    for by in range(1, cols):
        to_peer(by).wait_send()


def solution(mesh):
    slabs, cols = mesh.shape["slab"], mesh.shape["col"]

    def on_device(psi0, onsite, hop_x, hop_y, cos_coef, sin_coef):
        batch, rows, width = psi0.shape
        quarter = width // cols
        vmem = pl.BlockSpec(memory_space=pltpu.VMEM)
        hbm = pl.BlockSpec(memory_space=pltpu.HBM)
        f32 = jnp.float32
        return pl.pallas_call(
            functools.partial(kernel, slabs, cols),
            out_shape=jax.ShapeDtypeStruct((cos_coef.shape[0], 2, rows, quarter), f32),
            in_specs=[hbm] * 6,
            out_specs=vmem,
            scratch_shapes=[
                pltpu.VMEM((rows, width), f32),
                pltpu.VMEM((rows, width), f32),
                pltpu.VMEM((rows, width), f32),
                pltpu.SMEM(cos_coef.shape[::-1], f32),
                pltpu.SMEM(sin_coef.shape[::-1], f32),
                pltpu.SemaphoreType.DMA((5,)),
                pltpu.VMEM((batch, 8, width), jnp.bfloat16),
                pltpu.VMEM((4, width), f32),
                pltpu.VMEM((4, width), f32),
                pltpu.VMEM((4, width), f32),
                pltpu.VMEM((4, width), f32),
                pltpu.VMEM((3, 8, 8, width), f32),
                pltpu.VMEM((width // LANES, 64, LANES), f32),
                pltpu.VMEM((rows + 2, 8, width), f32),
                pltpu.VMEM((rows, 8, width), f32),
                pltpu.VMEM((3, rows, 8, width), f32),
                pltpu.VMEM((24, 8, width), f32),
                pltpu.VMEM((2, 8, width), f32),
                pltpu.VMEM((CHUNKS, 6, 8, width), f32),
                pltpu.VMEM((cols, 3, 8, quarter), f32),
                pltpu.VMEM((cols, 2, quarter), f32),
                pltpu.VMEM((cols - 1, 3, 8, quarter), f32),
                pltpu.VMEM((cols, 2, quarter), f32),
                pltpu.SemaphoreType.DMA((CHUNKS,)),
                pltpu.SemaphoreType.DMA((2, CHUNKS)),
                pltpu.SemaphoreType.DMA((2, CHUNKS)),
                pltpu.SemaphoreType.DMA((2,)),
                pltpu.SemaphoreType.DMA((2,)),
                pltpu.SemaphoreType.DMA((cols - 1,)),
                pltpu.SemaphoreType.DMA((cols - 1,)),
                pltpu.SemaphoreType.DMA((cols,)),
                pltpu.SemaphoreType.DMA((cols,)),
                pltpu.SemaphoreType.REGULAR((cols,)),
            ],
            compiler_params=pltpu.CompilerParams(
                collective_id=0, has_side_effects=True, vmem_limit_bytes=32 << 20),
        )(*(pltpu.with_memory_space_constraint(a, pltpu.HBM) for a in (
            psi0, onsite, hop_x, hop_y, cos_coef.T, sin_coef.T)))

    placed = (P("col", "slab", None), P("slab", None), P("slab", None), P("slab", None), P(), P())
    return jax.shard_map(
        on_device,
        mesh=mesh,
        in_specs=placed,
        out_specs=P(None, None, "slab", "col"),
        check_vma=False,
    )
```

```python
import functools

import jax
import jax.numpy as jnp
from jax import lax
from jax.experimental import pallas as pl
from jax.experimental.pallas import tpu as pltpu
from jax.sharding import PartitionSpec as P

MESH = pl.DeviceIdType.MESH
CHUNKS = 8
LANES = 128
AHEAD = 2


def kernel(slabs, cols, psi, onsite_hbm, hop_x_hbm, hop_y_hbm, cos_hbm, sin_hbm, out,
           onsite, hop_x, hop_y, cos_ref, sin_ref, input_sem, field, to_up, to_down, from_down, from_up, coef, states, first, second, beside, acc, sums, part, extra,
           got, got_extra, local_sem, send_sem, recv_sem, coef_send, coef_recv,
           part_send, part_recv, extra_send, extra_recv, go):
    slab = lax.axis_index("slab")
    col = lax.axis_index("col")
    batch, rows, width = psi.shape
    per = batch // CHUNKS
    quarter = width // cols
    has_down = slab > 0
    has_up = slab < slabs - 1

    def span(i):
        return pl.ds(i * per, per)

    def local(i):
        return pltpu.make_async_copy(
            psi.at[span(i)], field.at[span(i), 2:6, :], local_sem.at[i])

    def upward(i):
        return pltpu.make_async_remote_copy(
            src_ref=psi.at[span(i), 2:4, :], dst_ref=field.at[span(i), 0:2, :],
            send_sem=send_sem.at[0, i], recv_sem=recv_sem.at[0, i],
            device_id=(slab + 1, col), device_id_type=MESH)

    def downward(i):
        return pltpu.make_async_remote_copy(
            src_ref=psi.at[span(i), 0:2, :], dst_ref=field.at[span(i), 6:8, :],
            send_sem=send_sem.at[1, i], recv_sem=recv_sem.at[1, i],
            device_id=(slab - 1, col), device_id_type=MESH)

    coef_up = pltpu.make_async_remote_copy(
        src_ref=to_up, dst_ref=from_down, send_sem=coef_send.at[0],
        recv_sem=coef_recv.at[0], device_id=(slab + 1, col), device_id_type=MESH)
    coef_down = pltpu.make_async_remote_copy(
        src_ref=to_down, dst_ref=from_up, send_sem=coef_send.at[1],
        recv_sem=coef_recv.at[1], device_id=(slab - 1, col), device_id_type=MESH)

    place = lax.rem(slab, 4)
    is_0, is_1, is_2, is_3 = (place == n for n in range(4))

    def greet(sem_of, other):
        for by in range(cols):
            pl.semaphore_signal(sem_of, inc=1, device_id=(other, lax.rem(col + by, cols)),
                                device_id_type=MESH)

    barrier = pltpu.get_barrier_semaphore()

    @pl.when((is_0 | is_1) & has_up)
    def _():
        greet(barrier, slab + 1)

    @pl.when(jnp.logical_not(is_2) & has_down)
    def _():
        greet(barrier, slab - 1)

    @pl.when(is_2)
    def _():
        pl.semaphore_signal(barrier, inc=1, device_id=(slab - 1, col), device_id_type=MESH)

    @pl.when(jnp.logical_not(is_3))
    def _():
        for by in range(1, cols):
            pl.semaphore_signal(barrier, inc=1, device_id=(slab, lax.rem(col + by, cols)),
                                device_id_type=MESH)

    @pl.when(jnp.logical_not(is_3) | has_up)
    def _():
        pl.semaphore_wait(barrier, jnp.where(
            is_3, cols, jnp.where(is_2, 3 * cols - 1, jnp.where(is_1, 2 * cols, 2 * cols - 1))))

    def send_up(chunks):
        for i in chunks:
            upward(i).start()

    def send_down(chunks):
        for i in chunks:
            downward(i).start()

    ready_up = has_up
    ready_down = (is_1 | is_2) & has_down
    asked = (is_0 | is_3) & has_down

    @pl.when(ready_up)
    def _():
        send_up(range(AHEAD))

    @pl.when(ready_down)
    def _():
        send_down(range(AHEAD))

    @pl.when(is_2 | (is_3 & has_up))
    def _():
        for by in range(cols):
            pl.semaphore_signal(go.at[col], inc=1, device_id=(slab + 1, lax.rem(col + by, cols)),
                                device_id_type=MESH)

    loads = [
        pltpu.make_async_copy(source, target, input_sem.at[n])
        for n, (source, target) in enumerate((
            (hop_x_hbm, hop_x), (onsite_hbm, onsite), (hop_y_hbm, hop_y),
            (cos_hbm, cos_ref), (sin_hbm, sin_ref)))]
    for load in loads:
        load.start()
    for load in loads:
        load.wait()
    zero = jnp.zeros((1, width), jnp.float32)
    to_up[...] = jnp.concatenate(
        [hop_x[2:4, :], onsite[3:4, :], hop_y[3:4, :]], axis=0)
    to_down[...] = jnp.concatenate(
        [hop_x[0:1, :], onsite[0:1, :], hop_y[0:1, :], zero], axis=0)

    @pl.when(ready_up)
    def _():
        coef_up.start()
        send_up(range(AHEAD, CHUNKS))

    @pl.when(ready_down)
    def _():
        coef_down.start()
        send_down(range(AHEAD, CHUNKS))

    for i in range(CHUNKS):
        local(i).start()


    blank = jnp.zeros((batch, 2, width), jnp.bfloat16)

    @pl.when(jnp.logical_not(has_down))
    def _():
        field[:, 0:2, :] = blank
        from_down[...] = jnp.zeros_like(from_down)

    @pl.when(jnp.logical_not(has_up))
    def _():
        field[:, 6:8, :] = blank
        from_up[...] = jnp.zeros_like(from_up)

    acc[...] = jnp.zeros_like(acc)
    sums[...] = jnp.zeros_like(sums)

    @pl.when(asked)
    def _():
        pl.semaphore_wait(go.at[col], 1)
        send_down(range(AHEAD))
        coef_down.start()
        send_down(range(AHEAD, CHUNKS))

    @pl.when(has_down)
    def _():
        coef_up.wait_recv()

    @pl.when(has_up)
    def _():
        coef_down.wait_recv()

    low = from_down[...]
    high = from_up[...]
    site_x = jnp.concatenate([low[0:2], hop_x[...], high[0:1], zero], axis=0)
    site_on = jnp.concatenate([zero, low[2:3], onsite[...], high[1:2], zero], axis=0)
    site_y = jnp.concatenate([zero, low[3:4], hop_y[...], high[2:3], zero], axis=0)
    row_id = lax.broadcasted_iota(jnp.int32, (8, width), 0)
    lane_id = lax.broadcasted_iota(jnp.int32, (8, width), 1)
    site_x = jnp.where((row_id == 5) & jnp.logical_not(has_up), 0.0, site_x)
    bond_y = jnp.where((lax.rem(row_id + lane_id, 2) == 0) & (lane_id < width - 1), site_y, 0.0)
    both_y = bond_y + pltpu.roll(bond_y, 1, 1)
    for x in range(8):
        coef[0, x] = jnp.broadcast_to(site_on[x:x + 1], (8, width))
        coef[1, x] = jnp.broadcast_to(site_x[x:x + 1], (8, width))
        coef[2, x] = jnp.broadcast_to(both_y[x:x + 1], (8, width))

    lane = lax.broadcasted_iota(jnp.int32, (8, LANES), 1)
    odd_lane = lax.rem(lane, 2)
    near = (lane + 1 - 2 * odd_lane, lax.rem(lane + LANES - 1 + 2 * odd_lane, LANES))
    first_lane = lane == 0
    last_lane = lane == LANES - 1
    even_lane = odd_lane == 0
    tiles = width // LANES

    def partner(f, x):
        parts = [
            jnp.take_along_axis(f[:, k * LANES:(k + 1) * LANES], near[x % 2], axis=1)
            for k in range(tiles)]
        if x % 2:
            parts = [
                jnp.where(last_lane, parts[(k + 1) % tiles],
                          jnp.where(first_lane, parts[k - 1], parts[k]))
                for k in range(tiles)]
        return jnp.concatenate(parts, axis=1)

    def rounded(f):
        return f.astype(jnp.bfloat16).astype(jnp.float32)

    def load_states(g, start, stop):
        for c in range(8):
            block = field[g * 8 + c, start:stop, :].astype(jnp.float32)
            for k in range(tiles):
                states[k, 8 * c + start:8 * c + stop, :] = block[:, k * LANES:(k + 1) * LANES]

    def p_row(x):
        return jnp.concatenate(
            [states[k, pl.ds(x + 2, 8, stride=8), :] for k in range(tiles)], axis=1)

    def hamiltonian(row, x, side):
        return (coef[0, x + 2] * row(x) - coef[1, x + 1] * row(x - 1)
                - coef[1, x + 2] * row(x + 1) - coef[2, x + 2] * side)

    def vectors(g, start, stop, row_range, t_range):
        load_states(g, start, stop)
        for x in row_range:
            side = partner(p_row(x), x)
            if x in t_range:
                beside[0, x] = side
            first[x + 1] = rounded(hamiltonian(p_row, x, side))
        for x in t_range:
            side = partner(q_row(x), x)
            beside[1, x] = side
            t = rounded(2.0 * hamiltonian(q_row, x, side) - p_row(x))
            second[x] = t
            beside[2, x] = partner(t, x)

    def q_row(x):
        return first[x + 1]

    def lower_vectors(g):
        vectors(g, 0, 6, range(-1, 3), range(0, 2))
        sums[0] += p_row(-1) * second[0]
        sums[1] += q_row(-1) * second[0]

    def upper_vectors(g):
        vectors(g, 2, 8, range(1, rows + 1), range(2, rows))

    def rows_at(tile):
        lanes = pl.ds(pl.multiple_of(tile * LANES, LANES), LANES)

        def p(x):
            return states[tile, pl.ds(x + 2, 8, stride=8), :]

        def q(x):
            return first[x + 1, :, lanes]

        def t(x):
            return second[x, :, lanes]

        def add(n, value):
            acc[n, :, lanes] += value

        def across(h):
            x = 2 * h
            own = [jnp.where(even_lane, row(x), row(x + 1)) for row in (p, q, t)]
            side = [
                jnp.where(even_lane, beside[n, x, :, lanes], beside[n, x + 1, :, lanes])
                for n in range(3)]
            add(12 + h, own[0] * side[1] - own[1] * side[0])
            add(14 + h, own[0] * side[2] - own[2] * side[0])
            add(16 + h, own[1] * side[2] - own[2] * side[1])

        return p, q, t, add, across

    def lower_products(tile):
        p, q, t, add, across = rows_at(tile)
        for x in range(2):
            add(x, p(x) * q(x + 1) - q(x) * p(x + 1))
        add(4, p(0) * t(1) - t(0) * p(1))
        add(8, q(0) * t(1) - t(0) * q(1))
        add(5, -t(1) * p(2))
        add(9, -t(1) * q(2))
        across(0)

    def upper_products(tile):
        p, q, t, add, across = rows_at(tile)
        for x in range(2, 4):
            add(x, p(x) * q(x + 1) - q(x) * p(x + 1))
        add(5, p(1) * t(2))
        add(9, q(1) * t(2))
        add(6, p(2) * t(3) - t(2) * p(3))
        add(10, q(2) * t(3) - t(2) * q(3))
        add(7, -t(3) * p(4))
        add(11, -t(3) * q(4))
        across(1)

    def to_peer(by):
        return pltpu.make_async_remote_copy(
            src_ref=part.at[by], dst_ref=got.at[by - 1], send_sem=part_send.at[by - 1],
            recv_sem=part_recv.at[by - 1], device_id=(slab, lax.rem(col + by, cols)),
            device_id_type=MESH)

    def to_below(by):
        peer = lax.rem(col + by, cols)
        return pltpu.make_async_remote_copy(
            src_ref=extra.at[peer], dst_ref=got_extra.at[by], send_sem=extra_send.at[by],
            recv_sem=extra_recv.at[by], device_id=(slab - 1, peer),
            device_id_type=MESH)

    def wait_lower(i):
        @pl.when(has_down)
        def _():
            upward(i).wait_recv()

    def wait_upper(i):
        @pl.when(has_up)
        def _():
            downward(i).wait_recv()

    def send_extra():
        @pl.when(asked)
        def _():
            for by in range(1, cols):
                pl.semaphore_wait(go.at[lax.rem(col + by, cols)], 1)

        @pl.when(has_down)
        def _():
            for n in range(2):
                total = jnp.sum(sums[n], axis=0, keepdims=True)
                for j in range(cols):
                    extra[j, n:n + 1] = total[:, j * quarter:(j + 1) * quarter]
            for by in (2, 1, 3, 0):
                to_below(by).start()

    fold_row = lax.broadcasted_iota(jnp.int32, (8, quarter), 0)

    def folded(maps):
        size = 4
        while size:
            upper_rows = lax.rem(fold_row // size, 2) == 1
            half = len(maps) // 2
            maps = [
                jnp.where(upper_rows, maps[n + half] + pltpu.roll(maps[n + half], size, 0),
                          maps[n] + pltpu.roll(maps[n], 8 - size, 0))
                for n in range(half)]
            size //= 2
        return maps[0]

    per_quarter = quarter // LANES

    def share_out(products):
        odd = lax.rem(col, 2)
        for by in (2, 3 - 2 * odd, 1 + 2 * odd, 0):
            peer = lax.rem(col + by, cols)
            there = pl.ds(pl.multiple_of(peer * quarter, quarter), quarter)
            for k in range(per_quarter):
                products(peer * per_quarter + k)
            maps = [acc[n, :, there] for n in range(18)]
            part[by, 0:8] = folded(maps[0:8])
            part[by, 8:16] = folded(maps[8:16])
            part[by, 16:18] = folded(maps[16:18] * 4)[0:2]
            if not (isinstance(by, int) and by == 0):
                to_peer(by).start()

    def lower_chunk(i):
        wait_lower(i)
        lower_vectors(i)
        for k in range(tiles):
            lower_products(k)

    def upper_chunk(i):
        wait_upper(i)
        upper_vectors(i)
        for k in range(tiles):
            upper_products(k)

    def sweep(count, *steps):
        def step(i, carry):
            for one in steps:
                one(i)
            return carry

        lax.fori_loop(0, count, step, 0)

    def here_now(i):
        local(i).wait()

    last = CHUNKS - 1

    @pl.when(is_0)
    def _():
        here_now(0)
        upper_chunk(0)
        sweep(last, lambda i: here_now(i + 1), lambda i: upper_chunk(i + 1), lower_chunk)
        wait_lower(last)
        lower_vectors(last)
        share_out(lower_products)
        send_extra()

    @pl.when(jnp.logical_not(is_0))
    def _():
        sweep(CHUNKS, here_now, lower_chunk)
        send_extra()
        sweep(last, upper_chunk)
        wait_upper(last)
        upper_vectors(last)
        share_out(upper_products)

    @pl.when(jnp.logical_not(has_up))
    def _():
        got_extra[...] = jnp.zeros_like(got_extra)

    for by in range(1, cols):
        to_peer(by).wait_recv()

    @pl.when(has_up)
    def _():
        for by in range(cols):
            to_below(by).wait_recv()

    here = pl.ds(pl.multiple_of(col * quarter, quarter), quarter)
    extra_sum = got_extra[0] + got_extra[1] + got_extra[2] + got_extra[3]
    own_x = hop_x[:, here]
    own_y = hop_y[:, here]
    row4 = lax.broadcasted_iota(jnp.int32, (4, quarter), 0)
    lane4 = lax.broadcasted_iota(jnp.int32, (4, quarter), 1)
    keep = (lax.rem(row4 + lane4, 2) == 0) & (lane4 + col * quarter < width - 1)
    own_y = jnp.where(keep, own_y, 0.0)
    along = []
    across = []
    total = part[0] + got[0] + got[1] + got[2]
    for k in range(3):
        a = total[4 * k:4 * k + 4]
        if k:
            a = a + jnp.where(row4 == 3, extra_sum[k - 1:k], 0.0)
        along.append(a * own_x)
        n = 12 + 2 * k
        b = jnp.where(row4 < 2, total[n:n + 1], total[n + 1:n + 2])
        across.append(b * own_y)
    for e in range(cos_ref.shape[1]):
        c0, c1, c2 = (cos_ref[n, e] for n in range(3))
        s0, s1, s2 = (sin_ref[n, e] for n in range(3))
        d = (c0 * s1 - c1 * s0, c0 * s2 - c2 * s0, c1 * s2 - c2 * s1)
        out[e, 0] = d[0] * along[0] + d[1] * along[1] + d[2] * along[2]
        out[e, 1] = d[0] * across[0] + d[1] * across[1] + d[2] * across[2]

    @pl.when(has_up)
    def _():
        coef_up.wait_send()
        for i in range(CHUNKS):
            upward(i).wait_send()

    @pl.when(has_down)
    def _():
        coef_down.wait_send()
        for i in range(CHUNKS):
            downward(i).wait_send()
        for by in range(cols):
            to_below(by).wait_send()

    for by in range(1, cols):
        to_peer(by).wait_send()


def solution(mesh):
    slabs, cols = mesh.shape["slab"], mesh.shape["col"]

    def on_device(psi0, onsite, hop_x, hop_y, cos_coef, sin_coef):
        batch, rows, width = psi0.shape
        quarter = width // cols
        vmem = pl.BlockSpec(memory_space=pltpu.VMEM)
        hbm = pl.BlockSpec(memory_space=pltpu.HBM)
        f32 = jnp.float32
        return pl.pallas_call(
            functools.partial(kernel, slabs, cols),
            out_shape=jax.ShapeDtypeStruct((cos_coef.shape[0], 2, rows, quarter), f32),
            in_specs=[hbm] * 6,
            out_specs=vmem,
            scratch_shapes=[
                pltpu.VMEM((rows, width), f32),
                pltpu.VMEM((rows, width), f32),
                pltpu.VMEM((rows, width), f32),
                pltpu.SMEM(cos_coef.shape[::-1], f32),
                pltpu.SMEM(sin_coef.shape[::-1], f32),
                pltpu.SemaphoreType.DMA((5,)),
                pltpu.VMEM((batch, 8, width), jnp.bfloat16),
                pltpu.VMEM((4, width), f32),
                pltpu.VMEM((4, width), f32),
                pltpu.VMEM((4, width), f32),
                pltpu.VMEM((4, width), f32),
                pltpu.VMEM((3, 8, 8, width), f32),
                pltpu.VMEM((width // LANES, 64, LANES), f32),
                pltpu.VMEM((rows + 2, 8, width), f32),
                pltpu.VMEM((rows, 8, width), f32),
                pltpu.VMEM((3, rows, 8, width), f32),
                pltpu.VMEM((18, 8, width), f32),
                pltpu.VMEM((2, 8, width), f32),
                pltpu.VMEM((cols, 18, quarter), f32),
                pltpu.VMEM((cols, 2, quarter), f32),
                pltpu.VMEM((cols - 1, 18, quarter), f32),
                pltpu.VMEM((cols, 2, quarter), f32),
                pltpu.SemaphoreType.DMA((CHUNKS,)),
                pltpu.SemaphoreType.DMA((2, CHUNKS)),
                pltpu.SemaphoreType.DMA((2, CHUNKS)),
                pltpu.SemaphoreType.DMA((2,)),
                pltpu.SemaphoreType.DMA((2,)),
                pltpu.SemaphoreType.DMA((cols - 1,)),
                pltpu.SemaphoreType.DMA((cols - 1,)),
                pltpu.SemaphoreType.DMA((cols,)),
                pltpu.SemaphoreType.DMA((cols,)),
                pltpu.SemaphoreType.REGULAR((cols,)),
            ],
            compiler_params=pltpu.CompilerParams(
                collective_id=0, has_side_effects=True, vmem_limit_bytes=32 << 20),
        )(*(pltpu.with_memory_space_constraint(a, pltpu.HBM) for a in (
            psi0, onsite, hop_x, hop_y, cos_coef.T, sin_coef.T)))

    placed = (P("col", "slab", None), P("slab", None), P("slab", None), P("slab", None), P(), P())
    return jax.shard_map(
        on_device,
        mesh=mesh,
        in_specs=placed,
        out_specs=P(None, None, "slab", "col"),
        check_vma=False,
    )
```

```python
import functools

import jax
import jax.numpy as jnp
from jax import lax
from jax.experimental import pallas as pl
from jax.experimental.pallas import tpu as pltpu
from jax.sharding import PartitionSpec as P

MESH = pl.DeviceIdType.MESH
CHUNKS = 8
LANES = 128
AHEAD = 2


def kernel(slabs, cols, psi, onsite_hbm, hop_x_hbm, hop_y_hbm, cos_hbm, sin_hbm, out,
           onsite, hop_x, hop_y, cos_ref, sin_ref, input_sem, field, to_up, to_down, from_down, from_up, coef, states, first, second, beside, acc, sums, kept, part, extra,
           got, got_extra, local_sem, send_sem, recv_sem, coef_send, coef_recv,
           part_send, part_recv, extra_send, extra_recv, go):
    slab = lax.axis_index("slab")
    col = lax.axis_index("col")
    batch, rows, width = psi.shape
    per = batch // CHUNKS
    quarter = width // cols
    has_down = slab > 0
    has_up = slab < slabs - 1

    def span(i):
        return pl.ds(i * per, per)

    def local(i):
        return pltpu.make_async_copy(
            psi.at[span(i)], field.at[span(i), 2:6, :], local_sem.at[i])

    def upward(i):
        return pltpu.make_async_remote_copy(
            src_ref=psi.at[span(i), 2:4, :], dst_ref=field.at[span(i), 0:2, :],
            send_sem=send_sem.at[0, i], recv_sem=recv_sem.at[0, i],
            device_id=(slab + 1, col), device_id_type=MESH)

    def downward(i):
        return pltpu.make_async_remote_copy(
            src_ref=psi.at[span(i), 0:2, :], dst_ref=field.at[span(i), 6:8, :],
            send_sem=send_sem.at[1, i], recv_sem=recv_sem.at[1, i],
            device_id=(slab - 1, col), device_id_type=MESH)

    coef_up = pltpu.make_async_remote_copy(
        src_ref=to_up, dst_ref=from_down, send_sem=coef_send.at[0],
        recv_sem=coef_recv.at[0], device_id=(slab + 1, col), device_id_type=MESH)
    coef_down = pltpu.make_async_remote_copy(
        src_ref=to_down, dst_ref=from_up, send_sem=coef_send.at[1],
        recv_sem=coef_recv.at[1], device_id=(slab - 1, col), device_id_type=MESH)

    place = lax.rem(slab, 4)
    is_0, is_1, is_2, is_3 = (place == n for n in range(4))

    def greet(sem_of, other):
        for by in range(cols):
            pl.semaphore_signal(sem_of, inc=1, device_id=(other, lax.rem(col + by, cols)),
                                device_id_type=MESH)

    barrier = pltpu.get_barrier_semaphore()

    @pl.when((is_0 | is_1) & has_up)
    def _():
        greet(barrier, slab + 1)

    @pl.when(jnp.logical_not(is_2) & has_down)
    def _():
        greet(barrier, slab - 1)

    @pl.when(is_2)
    def _():
        pl.semaphore_signal(barrier, inc=1, device_id=(slab - 1, col), device_id_type=MESH)

    @pl.when(jnp.logical_not(is_3))
    def _():
        for by in range(1, cols):
            pl.semaphore_signal(barrier, inc=1, device_id=(slab, lax.rem(col + by, cols)),
                                device_id_type=MESH)

    @pl.when(jnp.logical_not(is_3) | has_up)
    def _():
        pl.semaphore_wait(barrier, jnp.where(
            is_3, cols, jnp.where(is_2, 3 * cols - 1, jnp.where(is_1, 2 * cols, 2 * cols - 1))))

    def send_up(chunks):
        for i in chunks:
            upward(i).start()

    def send_down(chunks):
        for i in chunks:
            downward(i).start()

    ready_up = has_up
    ready_down = (is_1 | is_2) & has_down
    asked = (is_0 | is_3) & has_down

    @pl.when(ready_up)
    def _():
        send_up(range(AHEAD))

    @pl.when(ready_down)
    def _():
        send_down(range(AHEAD))

    @pl.when(is_2 | (is_3 & has_up))
    def _():
        for by in range(cols):
            pl.semaphore_signal(go.at[col], inc=1, device_id=(slab + 1, lax.rem(col + by, cols)),
                                device_id_type=MESH)

    loads = [
        pltpu.make_async_copy(source, target, input_sem.at[n])
        for n, (source, target) in enumerate((
            (hop_x_hbm, hop_x), (onsite_hbm, onsite), (hop_y_hbm, hop_y),
            (cos_hbm, cos_ref), (sin_hbm, sin_ref)))]
    for load in loads:
        load.start()
    for load in loads:
        load.wait()
    zero = jnp.zeros((1, width), jnp.float32)
    to_up[...] = jnp.concatenate(
        [hop_x[2:4, :], onsite[3:4, :], hop_y[3:4, :]], axis=0)
    to_down[...] = jnp.concatenate(
        [hop_x[0:1, :], onsite[0:1, :], hop_y[0:1, :], zero], axis=0)

    @pl.when(ready_up)
    def _():
        coef_up.start()
        send_up(range(AHEAD, CHUNKS))

    @pl.when(ready_down)
    def _():
        coef_down.start()
        send_down(range(AHEAD, CHUNKS))

    for i in range(CHUNKS):
        local(i).start()


    blank = jnp.zeros((batch, 2, width), jnp.bfloat16)

    @pl.when(jnp.logical_not(has_down))
    def _():
        field[:, 0:2, :] = blank
        from_down[...] = jnp.zeros_like(from_down)

    @pl.when(jnp.logical_not(has_up))
    def _():
        field[:, 6:8, :] = blank
        from_up[...] = jnp.zeros_like(from_up)

    acc[...] = jnp.zeros_like(acc)
    sums[...] = jnp.zeros_like(sums)

    @pl.when(asked)
    def _():
        pl.semaphore_wait(go.at[col], 1)
        send_down(range(AHEAD))
        coef_down.start()
        send_down(range(AHEAD, CHUNKS))

    @pl.when(has_down)
    def _():
        coef_up.wait_recv()

    @pl.when(has_up)
    def _():
        coef_down.wait_recv()

    low = from_down[...]
    high = from_up[...]
    site_x = jnp.concatenate([low[0:2], hop_x[...], high[0:1], zero], axis=0)
    site_on = jnp.concatenate([zero, low[2:3], onsite[...], high[1:2], zero], axis=0)
    site_y = jnp.concatenate([zero, low[3:4], hop_y[...], high[2:3], zero], axis=0)
    row_id = lax.broadcasted_iota(jnp.int32, (8, width), 0)
    lane_id = lax.broadcasted_iota(jnp.int32, (8, width), 1)
    site_x = jnp.where((row_id == 5) & jnp.logical_not(has_up), 0.0, site_x)
    bond_y = jnp.where((lax.rem(row_id + lane_id, 2) == 0) & (lane_id < width - 1), site_y, 0.0)
    both_y = bond_y + pltpu.roll(bond_y, 1, 1)
    for x in range(8):
        coef[0, x] = jnp.broadcast_to(site_on[x:x + 1], (8, width))
        coef[1, x] = jnp.broadcast_to(site_x[x:x + 1], (8, width))
        coef[2, x] = jnp.broadcast_to(both_y[x:x + 1], (8, width))

    lane = lax.broadcasted_iota(jnp.int32, (8, LANES), 1)
    odd_lane = lax.rem(lane, 2)
    near = (lane + 1 - 2 * odd_lane, lax.rem(lane + LANES - 1 + 2 * odd_lane, LANES))
    first_lane = lane == 0
    last_lane = lane == LANES - 1
    even_lane = odd_lane == 0
    tiles = width // LANES

    def partner(f, x):
        parts = [
            jnp.take_along_axis(f[:, k * LANES:(k + 1) * LANES], near[x % 2], axis=1)
            for k in range(tiles)]
        if x % 2:
            parts = [
                jnp.where(last_lane, parts[(k + 1) % tiles],
                          jnp.where(first_lane, parts[k - 1], parts[k]))
                for k in range(tiles)]
        return jnp.concatenate(parts, axis=1)

    def rounded(f):
        return f.astype(jnp.bfloat16).astype(jnp.float32)

    def load_states(g, start, stop):
        for c in range(8):
            block = field[g * 8 + c, start:stop, :].astype(jnp.float32)
            for k in range(tiles):
                states[k, 8 * c + start:8 * c + stop, :] = block[:, k * LANES:(k + 1) * LANES]

    def p_row(x):
        return jnp.concatenate(
            [states[k, pl.ds(x + 2, 8, stride=8), :] for k in range(tiles)], axis=1)

    def hamiltonian(row, x, side):
        return (coef[0, x + 2] * row(x) - coef[1, x + 1] * row(x - 1)
                - coef[1, x + 2] * row(x + 1) - coef[2, x + 2] * side)

    def vectors(g, start, stop, row_range, t_range, again):
        load_states(g, start, stop)
        for x in row_range:
            if again and x in (1, 2):
                first[x + 1] = kept[g, x - 1]
                if x in t_range:
                    beside[0, x] = kept[g, 2]
                continue
            side = partner(p_row(x), x)
            q = rounded(hamiltonian(p_row, x, side))
            first[x + 1] = q
            if x in t_range:
                beside[0, x] = side
            if x in (1, 2):
                kept[g, x - 1] = q
                if x not in t_range:
                    kept[g, 2] = side
        for x in t_range:
            side = partner(q_row(x), x)
            beside[1, x] = side
            t = rounded(2.0 * hamiltonian(q_row, x, side) - p_row(x))
            second[x] = t
            beside[2, x] = partner(t, x)

    def q_row(x):
        return first[x + 1]

    def lower_vectors(g, again):
        vectors(g, 0, 6, range(-1, 3), range(0, 2), again)
        sums[0] += p_row(-1) * second[0]
        sums[1] += q_row(-1) * second[0]

    def upper_vectors(g, again):
        vectors(g, 2, 8, range(1, rows + 1), range(2, rows), again)

    def rows_at(tile):
        lanes = pl.ds(pl.multiple_of(tile * LANES, LANES), LANES)

        def p(x):
            return states[tile, pl.ds(x + 2, 8, stride=8), :]

        def q(x):
            return first[x + 1, :, lanes]

        def t(x):
            return second[x, :, lanes]

        def add(n, value):
            acc[n, :, lanes] += value

        def across(h):
            x = 2 * h
            own = [jnp.where(even_lane, row(x), row(x + 1)) for row in (p, q, t)]
            side = [
                jnp.where(even_lane, beside[n, x, :, lanes], beside[n, x + 1, :, lanes])
                for n in range(3)]
            add(12 + h, own[0] * side[1] - own[1] * side[0])
            add(14 + h, own[0] * side[2] - own[2] * side[0])
            add(16 + h, own[1] * side[2] - own[2] * side[1])

        return p, q, t, add, across

    def lower_products(tile):
        p, q, t, add, across = rows_at(tile)
        for x in range(2):
            add(x, p(x) * q(x + 1) - q(x) * p(x + 1))
        add(4, p(0) * t(1) - t(0) * p(1))
        add(8, q(0) * t(1) - t(0) * q(1))
        add(5, -t(1) * p(2))
        add(9, -t(1) * q(2))
        across(0)

    def upper_products(tile):
        p, q, t, add, across = rows_at(tile)
        for x in range(2, 4):
            add(x, p(x) * q(x + 1) - q(x) * p(x + 1))
        add(5, p(1) * t(2))
        add(9, q(1) * t(2))
        add(6, p(2) * t(3) - t(2) * p(3))
        add(10, q(2) * t(3) - t(2) * q(3))
        add(7, -t(3) * p(4))
        add(11, -t(3) * q(4))
        across(1)

    def to_peer(by):
        return pltpu.make_async_remote_copy(
            src_ref=part.at[by], dst_ref=got.at[by - 1], send_sem=part_send.at[by - 1],
            recv_sem=part_recv.at[by - 1], device_id=(slab, lax.rem(col + by, cols)),
            device_id_type=MESH)

    def to_below(by):
        peer = lax.rem(col + by, cols)
        return pltpu.make_async_remote_copy(
            src_ref=extra.at[peer], dst_ref=got_extra.at[by], send_sem=extra_send.at[by],
            recv_sem=extra_recv.at[by], device_id=(slab - 1, peer),
            device_id_type=MESH)

    def wait_lower(i):
        @pl.when(has_down)
        def _():
            upward(i).wait_recv()

    def wait_upper(i):
        @pl.when(has_up)
        def _():
            downward(i).wait_recv()

    def send_extra():
        @pl.when(asked)
        def _():
            for by in range(1, cols):
                pl.semaphore_wait(go.at[lax.rem(col + by, cols)], 1)

        @pl.when(has_down)
        def _():
            for n in range(2):
                total = jnp.sum(sums[n], axis=0, keepdims=True)
                for j in range(cols):
                    extra[j, n:n + 1] = total[:, j * quarter:(j + 1) * quarter]
            for by in (2, 1, 3, 0):
                to_below(by).start()

    fold_row = lax.broadcasted_iota(jnp.int32, (8, quarter), 0)

    def folded(maps):
        size = 4
        while size:
            upper_rows = lax.rem(fold_row // size, 2) == 1
            half = len(maps) // 2
            maps = [
                jnp.where(upper_rows, maps[n + half] + pltpu.roll(maps[n + half], size, 0),
                          maps[n] + pltpu.roll(maps[n], 8 - size, 0))
                for n in range(half)]
            size //= 2
        return maps[0]

    per_quarter = quarter // LANES

    def share_out(products):
        odd = lax.rem(col, 2)
        for by in (3 - odd, 2 - odd, 1 + 2 * odd, 0):
            peer = lax.rem(col + by, cols)
            there = pl.ds(pl.multiple_of(peer * quarter, quarter), quarter)
            for k in range(per_quarter):
                products(peer * per_quarter + k)
            maps = [acc[n, :, there] for n in range(18)]
            part[by, 0:8] = folded(maps[0:8])
            part[by, 8:16] = folded(maps[8:16])
            part[by, 16:18] = folded(maps[16:18] * 4)[0:2]
            if not (isinstance(by, int) and by == 0):
                to_peer(by).start()

    def lower_chunk(i, again):
        wait_lower(i)
        lower_vectors(i, again)
        for k in range(tiles):
            lower_products(k)

    def upper_chunk(i, again):
        wait_upper(i)
        upper_vectors(i, again)
        for k in range(tiles):
            upper_products(k)

    def sweep(count, *steps):
        def step(i, carry):
            for one in steps:
                one(i)
            return carry

        lax.fori_loop(0, count, step, 0)

    def here_now(i):
        local(i).wait()

    last = CHUNKS - 1

    @pl.when(is_0)
    def _():
        here_now(0)
        upper_chunk(0, False)
        sweep(last, lambda i: here_now(i + 1), lambda i: upper_chunk(i + 1, False),
              lambda i: lower_chunk(i, True))
        wait_lower(last)
        lower_vectors(last, True)
        share_out(lower_products)
        send_extra()

    @pl.when(jnp.logical_not(is_0))
    def _():
        sweep(CHUNKS, here_now, lambda i: lower_chunk(i, False))
        send_extra()
        sweep(last, lambda i: upper_chunk(i, True))
        wait_upper(last)
        upper_vectors(last, True)
        share_out(upper_products)

    @pl.when(jnp.logical_not(has_up))
    def _():
        got_extra[...] = jnp.zeros_like(got_extra)

    for by in range(1, cols):
        to_peer(by).wait_recv()

    @pl.when(has_up)
    def _():
        for by in range(cols):
            to_below(by).wait_recv()

    here = pl.ds(pl.multiple_of(col * quarter, quarter), quarter)
    extra_sum = got_extra[0] + got_extra[1] + got_extra[2] + got_extra[3]
    own_x = hop_x[:, here]
    own_y = hop_y[:, here]
    row4 = lax.broadcasted_iota(jnp.int32, (4, quarter), 0)
    lane4 = lax.broadcasted_iota(jnp.int32, (4, quarter), 1)
    keep = (lax.rem(row4 + lane4, 2) == 0) & (lane4 + col * quarter < width - 1)
    own_y = jnp.where(keep, own_y, 0.0)
    along = []
    across = []
    total = part[0] + got[0] + got[1] + got[2]
    for k in range(3):
        a = total[4 * k:4 * k + 4]
        if k:
            a = a + jnp.where(row4 == 3, extra_sum[k - 1:k], 0.0)
        along.append(a * own_x)
        n = 12 + 2 * k
        b = jnp.where(row4 < 2, total[n:n + 1], total[n + 1:n + 2])
        across.append(b * own_y)
    for e in range(cos_ref.shape[1]):
        c0, c1, c2 = (cos_ref[n, e] for n in range(3))
        s0, s1, s2 = (sin_ref[n, e] for n in range(3))
        d = (c0 * s1 - c1 * s0, c0 * s2 - c2 * s0, c1 * s2 - c2 * s1)
        out[e, 0] = d[0] * along[0] + d[1] * along[1] + d[2] * along[2]
        out[e, 1] = d[0] * across[0] + d[1] * across[1] + d[2] * across[2]

    @pl.when(has_up)
    def _():
        coef_up.wait_send()
        for i in range(CHUNKS):
            upward(i).wait_send()

    @pl.when(has_down)
    def _():
        coef_down.wait_send()
        for i in range(CHUNKS):
            downward(i).wait_send()
        for by in range(cols):
            to_below(by).wait_send()

    for by in range(1, cols):
        to_peer(by).wait_send()


def solution(mesh):
    slabs, cols = mesh.shape["slab"], mesh.shape["col"]

    def on_device(psi0, onsite, hop_x, hop_y, cos_coef, sin_coef):
        batch, rows, width = psi0.shape
        quarter = width // cols
        vmem = pl.BlockSpec(memory_space=pltpu.VMEM)
        hbm = pl.BlockSpec(memory_space=pltpu.HBM)
        f32 = jnp.float32
        return pl.pallas_call(
            functools.partial(kernel, slabs, cols),
            out_shape=jax.ShapeDtypeStruct((cos_coef.shape[0], 2, rows, quarter), f32),
            in_specs=[hbm] * 6,
            out_specs=vmem,
            scratch_shapes=[
                pltpu.VMEM((rows, width), f32),
                pltpu.VMEM((rows, width), f32),
                pltpu.VMEM((rows, width), f32),
                pltpu.SMEM(cos_coef.shape[::-1], f32),
                pltpu.SMEM(sin_coef.shape[::-1], f32),
                pltpu.SemaphoreType.DMA((5,)),
                pltpu.VMEM((batch, 8, width), jnp.bfloat16),
                pltpu.VMEM((4, width), f32),
                pltpu.VMEM((4, width), f32),
                pltpu.VMEM((4, width), f32),
                pltpu.VMEM((4, width), f32),
                pltpu.VMEM((3, 8, 8, width), f32),
                pltpu.VMEM((width // LANES, 64, LANES), f32),
                pltpu.VMEM((rows + 2, 8, width), f32),
                pltpu.VMEM((rows, 8, width), f32),
                pltpu.VMEM((3, rows, 8, width), f32),
                pltpu.VMEM((18, 8, width), f32),
                pltpu.VMEM((2, 8, width), f32),
                pltpu.VMEM((CHUNKS, 3, 8, width), f32),
                pltpu.VMEM((cols, 18, quarter), f32),
                pltpu.VMEM((cols, 2, quarter), f32),
                pltpu.VMEM((cols - 1, 18, quarter), f32),
                pltpu.VMEM((cols, 2, quarter), f32),
                pltpu.SemaphoreType.DMA((CHUNKS,)),
                pltpu.SemaphoreType.DMA((2, CHUNKS)),
                pltpu.SemaphoreType.DMA((2, CHUNKS)),
                pltpu.SemaphoreType.DMA((2,)),
                pltpu.SemaphoreType.DMA((2,)),
                pltpu.SemaphoreType.DMA((cols - 1,)),
                pltpu.SemaphoreType.DMA((cols - 1,)),
                pltpu.SemaphoreType.DMA((cols,)),
                pltpu.SemaphoreType.DMA((cols,)),
                pltpu.SemaphoreType.REGULAR((cols,)),
            ],
            compiler_params=pltpu.CompilerParams(
                collective_id=0, has_side_effects=True, vmem_limit_bytes=32 << 20),
        )(*(pltpu.with_memory_space_constraint(a, pltpu.HBM) for a in (
            psi0, onsite, hop_x, hop_y, cos_coef.T, sin_coef.T)))

    placed = (P("col", "slab", None), P("slab", None), P("slab", None), P("slab", None), P(), P())
    return jax.shard_map(
        on_device,
        mesh=mesh,
        in_specs=placed,
        out_specs=P(None, None, "slab", "col"),
        check_vma=False,
    )
```

```python
import functools

import jax
import jax.numpy as jnp
from jax import lax
from jax.experimental import pallas as pl
from jax.experimental.pallas import tpu as pltpu
from jax.sharding import PartitionSpec as P

MESH = pl.DeviceIdType.MESH
CHUNKS = 8
LANES = 128
AHEAD = 1


def kernel(slabs, cols, psi, onsite_hbm, hop_x_hbm, hop_y_hbm, cos_hbm, sin_hbm, out,
           onsite, hop_x, hop_y, cos_ref, sin_ref, input_sem, field, to_up, to_down, from_down, from_up, coef, states, first, second, beside, acc, sums, kept, part, extra,
           got, got_extra, local_sem, send_sem, recv_sem, coef_send, coef_recv,
           part_send, part_recv, extra_send, extra_recv, go):
    slab = lax.axis_index("slab")
    col = lax.axis_index("col")
    batch, rows, width = psi.shape
    per = batch // CHUNKS
    quarter = width // cols
    has_down = slab > 0
    has_up = slab < slabs - 1

    def span(i):
        return pl.ds(i * per, per)

    def local(i):
        return pltpu.make_async_copy(
            psi.at[span(i)], field.at[span(i), 2:6, :], local_sem.at[i])

    def upward(i):
        return pltpu.make_async_remote_copy(
            src_ref=psi.at[span(i), 2:4, :], dst_ref=field.at[span(i), 0:2, :],
            send_sem=send_sem.at[0, i], recv_sem=recv_sem.at[0, i],
            device_id=(slab + 1, col), device_id_type=MESH)

    def downward(i):
        return pltpu.make_async_remote_copy(
            src_ref=psi.at[span(i), 0:2, :], dst_ref=field.at[span(i), 6:8, :],
            send_sem=send_sem.at[1, i], recv_sem=recv_sem.at[1, i],
            device_id=(slab - 1, col), device_id_type=MESH)

    coef_up = pltpu.make_async_remote_copy(
        src_ref=to_up, dst_ref=from_down, send_sem=coef_send.at[0],
        recv_sem=coef_recv.at[0], device_id=(slab + 1, col), device_id_type=MESH)
    coef_down = pltpu.make_async_remote_copy(
        src_ref=to_down, dst_ref=from_up, send_sem=coef_send.at[1],
        recv_sem=coef_recv.at[1], device_id=(slab - 1, col), device_id_type=MESH)

    place = lax.rem(slab, 4)
    is_0, is_1, is_2, is_3 = (place == n for n in range(4))

    def greet(sem_of, other):
        for by in range(cols):
            pl.semaphore_signal(sem_of, inc=1, device_id=(other, lax.rem(col + by, cols)),
                                device_id_type=MESH)

    barrier = pltpu.get_barrier_semaphore()

    @pl.when((is_0 | is_1) & has_up)
    def _():
        greet(barrier, slab + 1)

    @pl.when(jnp.logical_not(is_2) & has_down)
    def _():
        greet(barrier, slab - 1)

    @pl.when(is_2)
    def _():
        pl.semaphore_signal(barrier, inc=1, device_id=(slab - 1, col), device_id_type=MESH)

    @pl.when(jnp.logical_not(is_3))
    def _():
        for by in range(1, cols):
            pl.semaphore_signal(barrier, inc=1, device_id=(slab, lax.rem(col + by, cols)),
                                device_id_type=MESH)

    @pl.when(jnp.logical_not(is_3) | has_up)
    def _():
        pl.semaphore_wait(barrier, jnp.where(
            is_3, cols, jnp.where(is_2, 3 * cols - 1, jnp.where(is_1, 2 * cols, 2 * cols - 1))))

    def send_up(chunks):
        for i in chunks:
            upward(i).start()

    def send_down(chunks):
        for i in chunks:
            downward(i).start()

    ready_up = has_up
    ready_down = (is_1 | is_2) & has_down
    asked = (is_0 | is_3) & has_down

    @pl.when(ready_up)
    def _():
        send_up(range(AHEAD))

    @pl.when(ready_down)
    def _():
        send_down(range(AHEAD))

    @pl.when(is_2 | (is_3 & has_up))
    def _():
        for by in range(cols):
            pl.semaphore_signal(go.at[col], inc=1, device_id=(slab + 1, lax.rem(col + by, cols)),
                                device_id_type=MESH)

    loads = [
        pltpu.make_async_copy(source, target, input_sem.at[n])
        for n, (source, target) in enumerate((
            (hop_x_hbm, hop_x), (onsite_hbm, onsite), (hop_y_hbm, hop_y),
            (cos_hbm, cos_ref), (sin_hbm, sin_ref)))]
    for load in loads:
        load.start()
    for load in loads:
        load.wait()
    zero = jnp.zeros((1, width), jnp.float32)
    to_up[...] = jnp.concatenate(
        [hop_x[2:4, :], onsite[3:4, :], hop_y[3:4, :]], axis=0)
    to_down[...] = jnp.concatenate(
        [hop_x[0:1, :], onsite[0:1, :], hop_y[0:1, :], zero], axis=0)

    @pl.when(ready_up)
    def _():
        coef_up.start()
        send_up(range(AHEAD, CHUNKS))

    @pl.when(ready_down)
    def _():
        coef_down.start()
        send_down(range(AHEAD, CHUNKS))

    for i in range(CHUNKS):
        local(i).start()


    blank = jnp.zeros((batch, 2, width), jnp.bfloat16)

    @pl.when(jnp.logical_not(has_down))
    def _():
        field[:, 0:2, :] = blank
        from_down[...] = jnp.zeros_like(from_down)

    @pl.when(jnp.logical_not(has_up))
    def _():
        field[:, 6:8, :] = blank
        from_up[...] = jnp.zeros_like(from_up)

    acc[...] = jnp.zeros_like(acc)
    sums[...] = jnp.zeros_like(sums)

    @pl.when(asked)
    def _():
        pl.semaphore_wait(go.at[col], 1)
        send_down(range(AHEAD))
        coef_down.start()
        send_down(range(AHEAD, CHUNKS))

    @pl.when(has_down)
    def _():
        coef_up.wait_recv()

    @pl.when(has_up)
    def _():
        coef_down.wait_recv()

    low = from_down[...]
    high = from_up[...]
    site_x = jnp.concatenate([low[0:2], hop_x[...], high[0:1], zero], axis=0)
    site_on = jnp.concatenate([zero, low[2:3], onsite[...], high[1:2], zero], axis=0)
    site_y = jnp.concatenate([zero, low[3:4], hop_y[...], high[2:3], zero], axis=0)
    row_id = lax.broadcasted_iota(jnp.int32, (8, width), 0)
    lane_id = lax.broadcasted_iota(jnp.int32, (8, width), 1)
    site_x = jnp.where((row_id == 5) & jnp.logical_not(has_up), 0.0, site_x)
    bond_y = jnp.where((lax.rem(row_id + lane_id, 2) == 0) & (lane_id < width - 1), site_y, 0.0)
    both_y = bond_y + pltpu.roll(bond_y, 1, 1)
    for x in range(8):
        coef[0, x] = jnp.broadcast_to(site_on[x:x + 1], (8, width))
        coef[1, x] = jnp.broadcast_to(site_x[x:x + 1], (8, width))
        coef[2, x] = jnp.broadcast_to(both_y[x:x + 1], (8, width))

    lane = lax.broadcasted_iota(jnp.int32, (8, LANES), 1)
    odd_lane = lax.rem(lane, 2)
    near = (lane + 1 - 2 * odd_lane, lax.rem(lane + LANES - 1 + 2 * odd_lane, LANES))
    first_lane = lane == 0
    last_lane = lane == LANES - 1
    even_lane = odd_lane == 0
    tiles = width // LANES

    def partner(f, x):
        parts = [
            jnp.take_along_axis(f[:, k * LANES:(k + 1) * LANES], near[x % 2], axis=1)
            for k in range(tiles)]
        if x % 2:
            parts = [
                jnp.where(last_lane, parts[(k + 1) % tiles],
                          jnp.where(first_lane, parts[k - 1], parts[k]))
                for k in range(tiles)]
        return jnp.concatenate(parts, axis=1)

    def rounded(f):
        return f.astype(jnp.bfloat16).astype(jnp.float32)

    def load_states(g, start, stop):
        for c in range(8):
            block = field[g * 8 + c, start:stop, :].astype(jnp.float32)
            for k in range(tiles):
                states[k, 8 * c + start:8 * c + stop, :] = block[:, k * LANES:(k + 1) * LANES]

    def p_row(x):
        return jnp.concatenate(
            [states[k, pl.ds(x + 2, 8, stride=8), :] for k in range(tiles)], axis=1)

    def hamiltonian(row, x, side):
        return (coef[0, x + 2] * row(x) - coef[1, x + 1] * row(x - 1)
                - coef[1, x + 2] * row(x + 1) - coef[2, x + 2] * side)

    def vectors(g, start, stop, row_range, t_range, again):
        load_states(g, start, stop)
        for x in row_range:
            if again and x in (1, 2):
                first[x + 1] = kept[g, x - 1]
                if x in t_range:
                    beside[0, x] = kept[g, 2]
                continue
            side = partner(p_row(x), x)
            q = rounded(hamiltonian(p_row, x, side))
            first[x + 1] = q
            if x in t_range:
                beside[0, x] = side
            if x in (1, 2):
                kept[g, x - 1] = q
                if x not in t_range:
                    kept[g, 2] = side
        for x in t_range:
            side = partner(q_row(x), x)
            beside[1, x] = side
            t = rounded(2.0 * hamiltonian(q_row, x, side) - p_row(x))
            second[x] = t
            beside[2, x] = partner(t, x)

    def q_row(x):
        return first[x + 1]

    def lower_vectors(g, again):
        vectors(g, 0, 6, range(-1, 3), range(0, 2), again)
        sums[0] += p_row(-1) * second[0]
        sums[1] += q_row(-1) * second[0]

    def upper_vectors(g, again):
        vectors(g, 2, 8, range(1, rows + 1), range(2, rows), again)

    def rows_at(tile):
        lanes = pl.ds(pl.multiple_of(tile * LANES, LANES), LANES)

        def p(x):
            return states[tile, pl.ds(x + 2, 8, stride=8), :]

        def q(x):
            return first[x + 1, :, lanes]

        def t(x):
            return second[x, :, lanes]

        def add(n, value):
            acc[n, :, lanes] += value

        def across(h):
            x = 2 * h
            own = [jnp.where(even_lane, row(x), row(x + 1)) for row in (p, q, t)]
            side = [
                jnp.where(even_lane, beside[n, x, :, lanes], beside[n, x + 1, :, lanes])
                for n in range(3)]
            add(12 + h, own[0] * side[1] - own[1] * side[0])
            add(14 + h, own[0] * side[2] - own[2] * side[0])
            add(16 + h, own[1] * side[2] - own[2] * side[1])

        return p, q, t, add, across

    def lower_products(tile):
        p, q, t, add, across = rows_at(tile)
        for x in range(2):
            add(x, p(x) * q(x + 1) - q(x) * p(x + 1))
        add(4, p(0) * t(1) - t(0) * p(1))
        add(8, q(0) * t(1) - t(0) * q(1))
        add(5, -t(1) * p(2))
        add(9, -t(1) * q(2))
        across(0)

    def upper_products(tile):
        p, q, t, add, across = rows_at(tile)
        for x in range(2, 4):
            add(x, p(x) * q(x + 1) - q(x) * p(x + 1))
        add(5, p(1) * t(2))
        add(9, q(1) * t(2))
        add(6, p(2) * t(3) - t(2) * p(3))
        add(10, q(2) * t(3) - t(2) * q(3))
        add(7, -t(3) * p(4))
        add(11, -t(3) * q(4))
        across(1)

    def to_peer(by):
        return pltpu.make_async_remote_copy(
            src_ref=part.at[by], dst_ref=got.at[by - 1], send_sem=part_send.at[by - 1],
            recv_sem=part_recv.at[by - 1], device_id=(slab, lax.rem(col + by, cols)),
            device_id_type=MESH)

    def to_below(by):
        peer = lax.rem(col + by, cols)
        return pltpu.make_async_remote_copy(
            src_ref=extra.at[peer], dst_ref=got_extra.at[by], send_sem=extra_send.at[by],
            recv_sem=extra_recv.at[by], device_id=(slab - 1, peer),
            device_id_type=MESH)

    def wait_lower(i):
        @pl.when(has_down)
        def _():
            upward(i).wait_recv()

    def wait_upper(i):
        @pl.when(has_up)
        def _():
            downward(i).wait_recv()

    def send_extra():
        @pl.when(asked)
        def _():
            for by in range(1, cols):
                pl.semaphore_wait(go.at[lax.rem(col + by, cols)], 1)

        @pl.when(has_down)
        def _():
            for n in range(2):
                total = jnp.sum(sums[n], axis=0, keepdims=True)
                for j in range(cols):
                    extra[j, n:n + 1] = total[:, j * quarter:(j + 1) * quarter]
            for by in (2, 1, 3, 0):
                to_below(by).start()

    fold_row = lax.broadcasted_iota(jnp.int32, (8, quarter), 0)

    def folded(maps):
        size = 4
        while size:
            upper_rows = lax.rem(fold_row // size, 2) == 1
            half = len(maps) // 2
            maps = [
                jnp.where(upper_rows, maps[n + half] + pltpu.roll(maps[n + half], size, 0),
                          maps[n] + pltpu.roll(maps[n], 8 - size, 0))
                for n in range(half)]
            size //= 2
        return maps[0]

    per_quarter = quarter // LANES

    def share_out(products):
        odd = lax.rem(col, 2)
        for by in (3 - odd, 2 - odd, 1 + 2 * odd, 0):
            peer = lax.rem(col + by, cols)
            there = pl.ds(pl.multiple_of(peer * quarter, quarter), quarter)
            for k in range(per_quarter):
                products(peer * per_quarter + k)
            maps = [acc[n, :, there] for n in range(18)]
            part[by, 0:8] = folded(maps[0:8])
            part[by, 8:16] = folded(maps[8:16])
            part[by, 16:18] = folded(maps[16:18] * 4)[0:2]
            if not (isinstance(by, int) and by == 0):
                to_peer(by).start()

    def lower_chunk(i, again):
        wait_lower(i)
        lower_vectors(i, again)
        for k in range(tiles):
            lower_products(k)

    def upper_chunk(i, again):
        wait_upper(i)
        upper_vectors(i, again)
        for k in range(tiles):
            upper_products(k)

    def sweep(count, *steps):
        def step(i, carry):
            for one in steps:
                one(i)
            return carry

        lax.fori_loop(0, count, step, 0)

    def here_now(i):
        local(i).wait()

    last = CHUNKS - 1

    @pl.when(is_0)
    def _():
        here_now(0)
        upper_chunk(0, False)
        sweep(last, lambda i: here_now(i + 1), lambda i: upper_chunk(i + 1, False),
              lambda i: lower_chunk(i, True))
        wait_lower(last)
        lower_vectors(last, True)
        share_out(lower_products)
        send_extra()

    @pl.when(jnp.logical_not(is_0))
    def _():
        sweep(CHUNKS, here_now, lambda i: lower_chunk(i, False))
        send_extra()
        sweep(last, lambda i: upper_chunk(i, True))
        wait_upper(last)
        upper_vectors(last, True)
        share_out(upper_products)

    @pl.when(jnp.logical_not(has_up))
    def _():
        got_extra[...] = jnp.zeros_like(got_extra)

    for by in range(1, cols):
        to_peer(by).wait_recv()

    @pl.when(has_up)
    def _():
        for by in range(cols):
            to_below(by).wait_recv()

    here = pl.ds(pl.multiple_of(col * quarter, quarter), quarter)
    extra_sum = got_extra[0] + got_extra[1] + got_extra[2] + got_extra[3]
    own_x = hop_x[:, here]
    own_y = hop_y[:, here]
    row4 = lax.broadcasted_iota(jnp.int32, (4, quarter), 0)
    lane4 = lax.broadcasted_iota(jnp.int32, (4, quarter), 1)
    keep = (lax.rem(row4 + lane4, 2) == 0) & (lane4 + col * quarter < width - 1)
    own_y = jnp.where(keep, own_y, 0.0)
    along = []
    across = []
    total = part[0] + got[0] + got[1] + got[2]
    for k in range(3):
        a = total[4 * k:4 * k + 4]
        if k:
            a = a + jnp.where(row4 == 3, extra_sum[k - 1:k], 0.0)
        along.append(a * own_x)
        n = 12 + 2 * k
        b = jnp.where(row4 < 2, total[n:n + 1], total[n + 1:n + 2])
        across.append(b * own_y)
    for e in range(cos_ref.shape[1]):
        c0, c1, c2 = (cos_ref[n, e] for n in range(3))
        s0, s1, s2 = (sin_ref[n, e] for n in range(3))
        d = (c0 * s1 - c1 * s0, c0 * s2 - c2 * s0, c1 * s2 - c2 * s1)
        out[e, 0] = d[0] * along[0] + d[1] * along[1] + d[2] * along[2]
        out[e, 1] = d[0] * across[0] + d[1] * across[1] + d[2] * across[2]

    @pl.when(has_up)
    def _():
        coef_up.wait_send()
        for i in range(CHUNKS):
            upward(i).wait_send()

    @pl.when(has_down)
    def _():
        coef_down.wait_send()
        for i in range(CHUNKS):
            downward(i).wait_send()
        for by in range(cols):
            to_below(by).wait_send()

    for by in range(1, cols):
        to_peer(by).wait_send()


def solution(mesh):
    slabs, cols = mesh.shape["slab"], mesh.shape["col"]

    def on_device(psi0, onsite, hop_x, hop_y, cos_coef, sin_coef):
        batch, rows, width = psi0.shape
        quarter = width // cols
        vmem = pl.BlockSpec(memory_space=pltpu.VMEM)
        hbm = pl.BlockSpec(memory_space=pltpu.HBM)
        f32 = jnp.float32
        return pl.pallas_call(
            functools.partial(kernel, slabs, cols),
            out_shape=jax.ShapeDtypeStruct((cos_coef.shape[0], 2, rows, quarter), f32),
            in_specs=[hbm] * 6,
            out_specs=vmem,
            scratch_shapes=[
                pltpu.VMEM((rows, width), f32),
                pltpu.VMEM((rows, width), f32),
                pltpu.VMEM((rows, width), f32),
                pltpu.SMEM(cos_coef.shape[::-1], f32),
                pltpu.SMEM(sin_coef.shape[::-1], f32),
                pltpu.SemaphoreType.DMA((5,)),
                pltpu.VMEM((batch, 8, width), jnp.bfloat16),
                pltpu.VMEM((4, width), f32),
                pltpu.VMEM((4, width), f32),
                pltpu.VMEM((4, width), f32),
                pltpu.VMEM((4, width), f32),
                pltpu.VMEM((3, 8, 8, width), f32),
                pltpu.VMEM((width // LANES, 64, LANES), f32),
                pltpu.VMEM((rows + 2, 8, width), f32),
                pltpu.VMEM((rows, 8, width), f32),
                pltpu.VMEM((3, rows, 8, width), f32),
                pltpu.VMEM((18, 8, width), f32),
                pltpu.VMEM((2, 8, width), f32),
                pltpu.VMEM((CHUNKS, 3, 8, width), f32),
                pltpu.VMEM((cols, 18, quarter), f32),
                pltpu.VMEM((cols, 2, quarter), f32),
                pltpu.VMEM((cols - 1, 18, quarter), f32),
                pltpu.VMEM((cols, 2, quarter), f32),
                pltpu.SemaphoreType.DMA((CHUNKS,)),
                pltpu.SemaphoreType.DMA((2, CHUNKS)),
                pltpu.SemaphoreType.DMA((2, CHUNKS)),
                pltpu.SemaphoreType.DMA((2,)),
                pltpu.SemaphoreType.DMA((2,)),
                pltpu.SemaphoreType.DMA((cols - 1,)),
                pltpu.SemaphoreType.DMA((cols - 1,)),
                pltpu.SemaphoreType.DMA((cols,)),
                pltpu.SemaphoreType.DMA((cols,)),
                pltpu.SemaphoreType.REGULAR((cols,)),
            ],
            compiler_params=pltpu.CompilerParams(
                collective_id=0, has_side_effects=True, vmem_limit_bytes=32 << 20),
        )(*(pltpu.with_memory_space_constraint(a, pltpu.HBM) for a in (
            psi0, onsite, hop_x, hop_y, cos_coef.T, sin_coef.T)))

    placed = (P("col", "slab", None), P("slab", None), P("slab", None), P("slab", None), P(), P())
    return jax.shard_map(
        on_device,
        mesh=mesh,
        in_specs=placed,
        out_specs=P(None, None, "slab", "col"),
        check_vma=False,
    )
```
